32 devices in a mesh: ctx: 32 (over z, y, x, core).
Axes of the slice: x: 2, y: 2, z: 4, core: 2. Of those that a mesh axis runs over, the one named last changes fastest.
Arguments:
- layer_input: bfloat16 [24576, 768], P('ctx'), may hold values from -6 to 6
- out_grad: bfloat16 [24576, 768], P('ctx'), may hold values from -6 to 6
- doc_starts: int32 [24], replicated, may hold values from 0 to 24576, as said below
- rand_blocks: int32 [384, 12, 3], P('ctx'), may hold values from 0 to 383, as said below
- query_weight: float32 [768, 768], P('ctx'), may hold values from -0.21875 to 0.21875
- query_bias: float32 [768], P('ctx'), may hold values from -1.8 to 1.8
- key_weight: float32 [768, 768], P('ctx'), may hold values from -0.21875 to 0.21875
- value_weight: float32 [768, 768], P('ctx'), may hold values from -0.21875 to 0.21875
- value_bias: float32 [768], P('ctx'), may hold values from -0.12 to 0.12
- output_weight: float32 [768, 768], P('ctx'), may hold values from -2.5 to 2.5
- output_bias: float32 [768], P('ctx'), may hold values from -1.2 to 1.2
- first_gain: float32 [768], P('ctx'), may hold values from 0.5 to 1.5
- first_shift: float32 [768], P('ctx'), may hold values from -1.2 to 1.2
- inner_weight: float32 [768, 3072], P('ctx'), may hold values from -0.21875 to 0.21875
- inner_bias: float32 [3072], P('ctx'), may hold values from -1.2 to 1.2
- outer_weight: float32 [3072, 768], P('ctx'), may hold values from -0.109375 to 0.109375
- outer_bias: float32 [768], P('ctx'), may hold values from -1.2 to 1.2
- second_gain: float32 [768], P('ctx'), may hold values from 0.5 to 1.5
- second_shift: float32 [768], P('ctx'), may hold values from -1.2 to 1.2
Outputs:
- layer_out: bfloat16 [24576, 768], P('ctx')
- grad_input: float32 [24576, 768], P('ctx')
- grad_query_weight: float32 [768, 768], P('ctx')
- grad_query_bias: float32 [768], P('ctx')
- grad_key_weight: float32 [768, 768], P('ctx')
- grad_value_weight: float32 [768, 768], P('ctx')
- grad_value_bias: float32 [768], P('ctx')
- grad_output_weight: float32 [768, 768], P('ctx')
- grad_output_bias: float32 [768], P('ctx')
- grad_first_gain: float32 [768], P('ctx')
- grad_first_shift: float32 [768], P('ctx')
- grad_inner_weight: float32 [768, 3072], P('ctx')
- grad_inner_bias: float32 [3072], P('ctx')
- grad_outer_weight: float32 [3072, 768], P('ctx')
- grad_outer_bias: float32 [768], P('ctx')
- grad_second_gain: float32 [768], P('ctx')
- grad_second_shift: float32 [768], P('ctx')
The draws below stay inside these ranges and needn't reach their ends.
Inputs may be any that keep to these rules, and one draw needn't show every extreme that they name: `doc_starts`: ascending multiples of 64, the first 0. The entries below 24576 cut the stream into documents of 16 to 32 blocks, one of exactly 32 and one of exactly 16 blocks; every remaining entry at the end equals 24576. rand_blocks[b, h, :] are 3 different blocks of the document of block b, none within one block of b and none among the document's first two blocks. Rows of a document's first two blocks are not read.
All inputs are finite; a program needn't handle non-finite values.
Results may differ from the reference program's by a relative error of at most 0.014.
The reference program's roundings to bfloat16 on the way count: a program that leaves them out, or rounds other values in their place, can miss the bound.
Values may be sent and summed in bfloat16 or wider, within the bound.
A program may use at most 144 MiB of HBM per device.

```python
import math
import jax
import jax.numpy as jnp
from jax import lax

D = 768
HEADS = 12
HEAD_DIM = 64
FF = 3072
BLOCK = 64
RANDOM = 3
DOC_MIN = 16
DOC_MAX = 32
TOKENS = 24576


def doc_layout(key):
    block_count = TOKENS // BLOCK
    slots_total = block_count // DOC_MIN
    doc_gaps = jax.random.randint(jax.random.fold_in(key, 11), (slots_total,), DOC_MIN, DOC_MAX + 1)
    max_place = jax.random.randint(jax.random.fold_in(key, 12), (), 0, 4)
    indices = jnp.arange(slots_total)
    doc_gaps = jnp.where(indices == max_place, DOC_MAX, doc_gaps)
    doc_gaps = jnp.where(indices == max_place + 1, DOC_MIN, doc_gaps)
    starts = jnp.concatenate([jnp.zeros((1,), jnp.int32), jnp.cumsum(doc_gaps)[:-1].astype(jnp.int32)])
    usable = starts <= block_count - DOC_MIN
    last_start = jnp.max(jnp.where(usable, starts, 0))
    leftover = block_count - last_start
    split_at = jnp.where(leftover > DOC_MAX, last_start + leftover // 2, block_count).astype(jnp.int32)
    used_count = jnp.sum(usable.astype(jnp.int32))
    starts = jnp.where(usable, starts, block_count).astype(jnp.int32)
    return starts.at[used_count].set(split_at, mode='drop')


def draw_doc_starts(key, part):
    return (doc_layout(jax.random.fold_in(key, 5)) * BLOCK).astype(jnp.int32)


def draw_rand_blocks(key, part):
    block_count = TOKENS // BLOCK
    starts = doc_layout(jax.random.fold_in(key, 5))
    bounds = jnp.concatenate([starts, jnp.full((1,), block_count, jnp.int32)])
    blocks = jnp.arange(block_count, dtype=jnp.int32)
    before = starts[None, :] <= blocks[:, None]
    doc_ids = jnp.sum(before.astype(jnp.int32), axis=1) - 1
    first_block = bounds[doc_ids]
    length = bounds[doc_ids + 1] - first_block
    offsets = jnp.arange(DOC_MAX, dtype=jnp.int32)
    candidate = first_block[:, None] + offsets[None, :]
    usable = (offsets[None, :] < length[:, None]) & (jnp.abs(candidate - blocks[:, None]) > 1) & (offsets[None, :] >= 2)
    rank_draw = jax.random.randint(jax.random.fold_in(key, 7), (block_count, HEADS, DOC_MAX), 0, 1 << 20)
    scores = jnp.where(usable[:, None, :], rank_draw * DOC_MAX + offsets[None, None, :], -1)
    chosen = lax.top_k(scores, RANDOM)[1]
    return (first_block[:, None, None] + chosen).astype(jnp.int32)


def raised(drawn, own_key, source, target, blocks, factor):
    owner, partner = [(jnp.arange(drawn.shape[position]) // (drawn.shape[position] // blocks)).reshape([-1 if axis == position else 1 for axis in range(drawn.ndim)]) for position in (source, target)]
    chosen = jax.random.permutation(own_key, blocks)[partner]
    strong = (owner == chosen) | (owner == (partner + blocks // 2) % blocks)
    return jnp.where(strong, factor * drawn, drawn)


def shard_levels(rng, extent, cuts, smallest, top_value):
    loudness = 1.0
    for dim, blocks in cuts:
        heights = jax.random.uniform(jax.random.fold_in(jax.random.fold_in(rng, 6), dim), (blocks,), jnp.float32, smallest / len(cuts), top_value / len(cuts))
        loudness = loudness * jnp.repeat(jnp.exp(heights), extent[dim] // blocks).reshape((-1,) + (1,) * (len(extent) - 1 - dim))
    return loudness


def bell_draw(rng, dims, deviation, reach, cuts=(), kind=jnp.bfloat16):
    result = deviation * jax.random.normal(rng, dims, jnp.float32)
    if cuts:
        result = result * shard_levels(rng, dims, cuts, -0.22, 0.18)
    return jnp.clip(result, -reach, reach).astype(kind)


def noise_with(key, extent, scale, limit, split, heavy, kind=jnp.bfloat16):
    array = scale * jax.random.normal(key, extent, jnp.float32)
    if split:
        array = array * shard_levels(key, extent, split, -0.22, 0.18)
    return jnp.clip(raised(array, jax.random.fold_in(key, 3), *heavy), -limit, limit).astype(kind)


def setup_inputs(seed: int = 0) -> dict:
    key_list = jax.random.split(jax.random.key(seed), 20)
    return {
        "layer_input": noise_with(key_list[0], (TOKENS, D), 1.0, 6.0, ((0, 32),), (0, 1, 32, 2.75)),
        "out_grad": noise_with(key_list[1], (TOKENS, D), 1.0, 6.0, ((0, 32),), (0, 1, 32, 2.75)),
        "doc_starts": draw_doc_starts(jax.random.fold_in(key_list[19], 71), 0),
        "rand_blocks": draw_rand_blocks(jax.random.fold_in(key_list[19], 71), 0),
        "query_weight": bell_draw(key_list[4], (D, D), D ** -0.5, 0.21875, ((0, 32),), jnp.float32),
        "query_bias": bell_draw(key_list[5], (D,), 0.3, 1.8, ((0, 32),), jnp.float32),
        "key_weight": bell_draw(key_list[6], (D, D), D ** -0.5, 0.21875, ((0, 32),), jnp.float32),
        "value_weight": bell_draw(key_list[7], (D, D), D ** -0.5, 0.21875, ((0, 32),), jnp.float32),
        "value_bias": bell_draw(key_list[8], (D,), 0.02, 0.12, ((0, 32),), jnp.float32),
        "output_weight": bell_draw(key_list[9], (D, D), (D * D // (1536 * BLOCK)) ** -0.5, 2.5, ((0, 32),), jnp.float32),
        "output_bias": bell_draw(key_list[10], (D,), 0.2, 1.2, ((0, 32),), jnp.float32),
        "first_gain": jnp.clip(1.0 + 0.1 * jax.random.normal(key_list[11], (D,), jnp.float32), 0.5, 1.5),
        "first_shift": bell_draw(key_list[12], (D,), 0.2, 1.2, ((0, 32),), jnp.float32),
        "inner_weight": bell_draw(key_list[13], (D, FF), D ** -0.5, 0.21875, ((0, 32),), jnp.float32),
        "inner_bias": bell_draw(key_list[14], (FF,), 0.2, 1.2, ((0, 32),), jnp.float32),
        "outer_weight": bell_draw(key_list[15], (FF, D), FF ** -0.5, 0.109375, ((0, 32),), jnp.float32),
        "outer_bias": bell_draw(key_list[16], (D,), 0.2, 1.2, ((0, 32),), jnp.float32),
        "second_gain": jnp.clip(1.0 + 0.1 * jax.random.normal(key_list[17], (D,), jnp.float32), 0.5, 1.5),
        "second_shift": bell_draw(key_list[18], (D,), 0.2, 1.2, ((0, 32),), jnp.float32),
    }


norm_eps = 1e-06

@jax.custom_vjp
def low(v):
    return lax.optimization_barrier(v.astype(jnp.bfloat16)).astype(jnp.float32)

@jax.custom_vjp
def low_back(v):
    return v

def low_keep(v):
    return (low(v), None)

def low_pass(kept, grad):
    return (grad,)

def back_keep(v):
    return (v, None)

def back_low(kept, grad):
    return (low(grad),)
low.defvjp(low_keep, low_pass)
low_back.defvjp(back_keep, back_low)

def exact_dot(left, right):
    return jnp.dot(left, right, precision=lax.Precision.HIGHEST, preferred_element_type=jnp.float32)

def layer_norm(hidden, scale_gain, shift_vec):
    row_mean = lax.optimization_barrier(jnp.mean(hidden, axis=-1, keepdims=True))
    centred = hidden - row_mean
    variance = lax.optimization_barrier(jnp.mean(centred * centred, axis=-1, keepdims=True))
    return centred * lax.rsqrt(variance + norm_eps) * scale_gain + shift_vec

def block_layout(doc_starts):
    block_count = TOKENS // BLOCK
    blocks = jnp.arange(block_count, dtype=jnp.int32)
    start_blocks = (doc_starts // BLOCK).astype(jnp.int32)
    before = start_blocks[None, :] <= blocks[:, None]
    doc_ids = lax.optimization_barrier(jnp.sum(before.astype(jnp.int32), axis=1)) - 1
    first_block = lax.optimization_barrier(jnp.max(jnp.where(before, start_blocks[None, :], -1), axis=1))
    return (doc_ids.astype(jnp.int32), first_block.astype(jnp.int32))

def attend(query_rows, key_matrix, value_matrix, doc_ids, first_block, rand_blocks):
    block_count = TOKENS // BLOCK
    pad_blocks = DOC_MAX - 1
    window_blocks = 2 * DOC_MAX - 1
    score_scale = 1.0 / math.sqrt(HEAD_DIM)
    query_blocks = query_rows.reshape(block_count, BLOCK, HEADS, HEAD_DIM)
    pad_widths = ((pad_blocks, pad_blocks), (0, 0), (0, 0), (0, 0))
    key_pad = jnp.pad(key_matrix.reshape(block_count, BLOCK, HEADS, HEAD_DIM), pad_widths)
    value_pad = jnp.pad(value_matrix.reshape(block_count, BLOCK, HEADS, HEAD_DIM), pad_widths)
    doc_pad = jnp.pad(doc_ids, (pad_blocks, pad_blocks), constant_values=-1)

    @jax.checkpoint
    def one_block(block_index):
        near_keys = lax.dynamic_slice_in_dim(key_pad, block_index, window_blocks, 0).reshape(window_blocks * BLOCK, HEADS, HEAD_DIM)
        near_values = lax.dynamic_slice_in_dim(value_pad, block_index, window_blocks, 0).reshape(window_blocks * BLOCK, HEADS, HEAD_DIM)
        key_doc = lax.dynamic_slice_in_dim(doc_pad, block_index, window_blocks, 0)
        key_block = block_index - pad_blocks + jnp.arange(window_blocks, dtype=jnp.int32)
        own_first = first_block[block_index]
        same_doc = key_doc == doc_ids[block_index]
        near_mask = jnp.abs(key_block - block_index) <= 1
        global_key = (key_block == own_first) | (key_block == own_first + 1)
        random_key = jnp.any(key_block[None, :, None] == rand_blocks[block_index][:, None, :], axis=2)
        global_query = block_index - own_first < 2
        allowed = same_doc[None, :] & (global_query | near_mask[None, :] | global_key[None, :] | random_key)
        allowed = jnp.repeat(allowed, BLOCK, axis=1)
        raw_scores = jnp.einsum('qhd,khd->hqk', query_blocks[block_index], near_keys, precision=lax.Precision.HIGHEST)
        scores = low_back(raw_scores * score_scale)
        scores = jnp.where(allowed[:, None, :], scores, -1e+30)
        row_max = lax.optimization_barrier(jnp.max(scores, axis=-1, keepdims=True))
        weights = jnp.exp(scores - row_max)
        attention_probability = weights / lax.optimization_barrier(jnp.sum(weights, axis=-1, keepdims=True))
        return jnp.einsum('hqk,khd->qhd', low(attention_probability), near_values, precision=lax.Precision.HIGHEST)
    blocks_out = lax.map(one_block, jnp.arange(block_count, dtype=jnp.int32))
    return blocks_out.reshape(TOKENS, HEADS * HEAD_DIM)

def reference(layer_input, out_grad, doc_starts, rand_blocks, query_weight, query_bias, key_weight, value_weight, value_bias, output_weight, output_bias, first_gain, first_shift, inner_weight, inner_bias, outer_weight, outer_bias, second_gain, second_shift):
    doc_ids, first_block = block_layout(doc_starts)

    def forward(input_rows, params):
        w_query, b_query, w_key, w_value, b_value, w_output, b_output, g_first, s_first, w_inner, b_inner, w_outer, b_outer, g_second, s_second = [low(param) for param in params]
        query_rows = low_back(low(exact_dot(input_rows, w_query) + b_query))
        key_matrix = low_back(low(exact_dot(input_rows, w_key)))
        value_matrix = low_back(low(exact_dot(input_rows, w_value) + b_value))
        context_rows = low_back(low(attend(query_rows, key_matrix, value_matrix, doc_ids, first_block, rand_blocks)))
        resid_one = input_rows + low_back(exact_dot(context_rows, w_output) + b_output)
        normed_one = layer_norm(resid_one, g_first, s_first)
        inner_pre = low_back(exact_dot(low(normed_one), w_inner) + b_inner)
        active = low(jax.nn.gelu(inner_pre, approximate=False))
        resid_two = normed_one + low_back(exact_dot(active, w_outer) + b_outer)
        return layer_norm(resid_two, g_second, s_second)
    params = (query_weight, query_bias, key_weight, value_weight, value_bias, output_weight, output_bias, first_gain, first_shift, inner_weight, inner_bias, outer_weight, outer_bias, second_gain, second_shift)
    layer_out, pullback = jax.vjp(forward, layer_input.astype(jnp.float32), params)
    grad_input, gradients = pullback(out_grad.astype(jnp.float32))
    return (layer_out.astype(jnp.bfloat16), grad_input, gradients[0], gradients[1], gradients[2], gradients[3], gradients[4], gradients[5], gradients[6], gradients[7], gradients[8], gradients[9], gradients[10], gradients[11], gradients[12], gradients[13], gradients[14])
```

```python
import functools
import math

import jax
import jax.numpy as jnp
from jax import lax
from jax.experimental import pallas as pl
from jax.experimental.pallas import tpu as pltpu
from jax.sharding import PartitionSpec as P

BLOCK = 64
DOC_MAX = 32
REACH = DOC_MAX - 1
SLOTS = 8
WIDE = SLOTS * BLOCK
CHUNKS = DOC_MAX // SLOTS
LANES = 128

norm_eps = 1e-06
masked_score = -1e30
BF = jnp.bfloat16
F32 = jnp.float32


def passed_along(value, axis, steps):
    count = lax.axis_size(axis)
    first, last = (max(0, -steps), min(count, count - steps))
    return lax.ppermute(value, axis, [(source, source + steps) for source in range(first, last)])


def layer_norm(hidden, scale_gain, shift_vec):
    row_mean = jnp.mean(hidden, axis=-1, keepdims=True)
    centred = hidden - row_mean
    variance = jnp.mean(centred * centred, axis=-1, keepdims=True)
    return centred * lax.rsqrt(variance + norm_eps) * scale_gain + shift_vec


def gelu_exact(inner_pre):
    return jax.nn.gelu(inner_pre, approximate=False)


def plain_dot(left, right):
    return jnp.dot(left, right, preferred_element_type=F32)


def rows_dot(left, right):
    return lax.dot_general(left, right, (((0,), (0,)), ((), ())), preferred_element_type=F32)


def cols_dot(left, right):
    return lax.dot_general(left, right, (((1,), (1,)), ((), ())), preferred_element_type=F32)


def edge_rows(distance, own_blocks):
    return BLOCK * min(own_blocks, DOC_MAX - 1 - (distance - 1) * own_blocks)


def doc_layout(doc_starts, block_ids):
    start_blocks = doc_starts // BLOCK
    before = start_blocks[None, :] <= block_ids[:, None]
    doc_ids = jnp.sum(before.astype(jnp.int32), axis=1) - 1
    first_block = jnp.max(jnp.where(before, start_blocks[None, :], -1), axis=1)
    return (doc_ids, first_block)


def low_half():
    return lax.broadcasted_iota(jnp.int32, (BLOCK, LANES), 1) < LANES // 2


def split_pair(rows):
    half = low_half()
    zero = jnp.zeros_like(rows)
    return jnp.concatenate([jnp.where(half, rows, zero), jnp.where(half, zero, rows)], axis=0)


def join_pair(rows):
    return jnp.where(low_half(), rows[:BLOCK], rows[BLOCK:])


def block_at(ref, position):
    return ref[pl.ds(pl.multiple_of(position * BLOCK, BLOCK), BLOCK), :]


def slots_of(near_ref, rand_ref, block, pair, heads):
    shared = [near_ref[block * 8 + i] for i in range(5)]
    at = (block * heads + 2 * pair) * 3
    chosen = [(rand_ref[at + i], rand_ref[at + 3 + i]) for i in range(3)]
    return shared, chosen


def slot_rows(ref, shared, chosen):
    half = low_half()
    parts = [block_at(ref, i) for i in shared]
    parts += [jnp.where(half, block_at(ref, a), block_at(ref, b)) for a, b in chosen]
    return jnp.concatenate(parts, axis=0)


def slot_bias(near_ref, block):
    after = jnp.where(near_ref[block * 8 + 5] > 0, 0.0, masked_score).astype(F32)
    lead = jnp.where(near_ref[block * 8 + 6] > 0, 0.0, masked_score).astype(F32)
    return after, lead


def forward_kernel(heads, own_blocks, near_ref, rand_ref, glob_ref, q_ref, k_ref, v_ref, o_ref, s_ref):
    pair = pl.program_id(0)
    slot_id = lax.broadcasted_iota(jnp.int32, (1, WIDE), 1) // BLOCK

    def regular(block, carry):
        rows = pl.ds(pl.multiple_of(block * BLOCK, BLOCK), BLOCK)
        shared, chosen = slots_of(near_ref, rand_ref, block, pair, heads)
        queries = split_pair(q_ref[rows, :] * 0.125)
        scores = cols_dot(queries, slot_rows(k_ref, shared, chosen))
        after, lead = slot_bias(near_ref, block)
        scores = scores + jnp.where(slot_id == 2, after, jnp.where(slot_id == 4, lead, 0.0))
        weights = jnp.exp(scores - jnp.max(scores, axis=1, keepdims=True))
        probs = weights * (1.0 / jnp.sum(weights, axis=1, keepdims=True))
        mixed = plain_dot(probs.astype(BF), slot_rows(v_ref, shared, chosen))
        o_ref[rows, :] = join_pair(mixed).astype(BF)
        return carry

    lax.fori_loop(0, own_blocks, regular, 0, unroll=4)

    def whole(block, carry):
        @pl.when(glob_ref[block * 4] > 0)
        def _():
            rows = pl.ds(pl.multiple_of(block * BLOCK, BLOCK), BLOCK)
            first = glob_ref[block * 4 + 1]
            length = glob_ref[block * 4 + 2]
            chunks = (length + SLOTS - 1) // SLOTS
            queries = split_pair(q_ref[rows, :] * 0.125)

            def score(step, top):
                at = pl.ds(pl.multiple_of((first + step * SLOTS) * BLOCK, BLOCK), WIDE)
                scores = cols_dot(queries, k_ref[at, :])
                scores = jnp.where(slot_id < length - step * SLOTS, scores, masked_score)
                s_ref[step] = scores
                return jnp.maximum(top, jnp.max(scores, axis=1, keepdims=True))

            top = lax.fori_loop(0, chunks, score, jnp.full((LANES, 1), masked_score, F32))

            def mix(step, kept):
                total, acc = kept
                at = pl.ds(pl.multiple_of((first + step * SLOTS) * BLOCK, BLOCK), WIDE)
                weights = jnp.exp(s_ref[step] - top)
                return (
                    total + jnp.sum(weights, axis=1, keepdims=True),
                    acc + plain_dot(weights.astype(BF), v_ref[at, :]),
                )

            total, acc = lax.fori_loop(
                0, chunks, mix, (jnp.zeros((LANES, 1), F32), jnp.zeros((LANES, LANES), F32))
            )
            o_ref[rows, :] = join_pair(acc * (1.0 / total)).astype(BF)

        return carry

    lax.fori_loop(0, own_blocks, whole, 0)


def backward_kernel(
    heads, own_blocks, near_ref, rand_ref, glob_ref, q_ref, k_ref, v_ref, c_ref,
    dq_ref, dk_ref, dv_ref, dk_acc, dv_acc, s_ref, p_ref,
):
    pair = pl.program_id(0)
    dk_acc[...] = jnp.zeros_like(dk_acc)
    dv_acc[...] = jnp.zeros_like(dv_acc)
    half = low_half()

    def add_rows(acc, shared, chosen, update):
        for i, position in enumerate(shared):
            at = pl.ds(pl.multiple_of(position * BLOCK, BLOCK), BLOCK)
            acc[at, :] += update[i * BLOCK : (i + 1) * BLOCK]
        for i, (one, two) in enumerate(chosen):
            piece = update[(5 + i) * BLOCK : (6 + i) * BLOCK]
            at = pl.ds(pl.multiple_of(one * BLOCK, BLOCK), BLOCK)
            acc[at, :] += jnp.where(half, piece, 0.0)
            at = pl.ds(pl.multiple_of(two * BLOCK, BLOCK), BLOCK)
            acc[at, :] += jnp.where(half, 0.0, piece)

    def regular(block, carry):
        rows = pl.ds(pl.multiple_of(block * BLOCK, BLOCK), BLOCK)
        shared, chosen = slots_of(near_ref, rand_ref, block, pair, heads)
        queries = split_pair(q_ref[rows, :] * 0.125)
        slope = c_ref[rows, :]
        slope = split_pair(jnp.where(glob_ref[block * 4] > 0, jnp.zeros_like(slope), slope))
        keys = slot_rows(k_ref, shared, chosen)
        scores = cols_dot(keys, queries)
        after, lead = slot_bias(near_ref, block)
        scores = jnp.concatenate(
            [
                scores[: 2 * BLOCK],
                scores[2 * BLOCK : 3 * BLOCK] + after,
                scores[3 * BLOCK : 4 * BLOCK],
                scores[4 * BLOCK : 5 * BLOCK] + lead,
                scores[5 * BLOCK :],
            ],
            axis=0,
        )
        weights = jnp.exp(scores - jnp.max(scores, axis=0, keepdims=True))
        probs = weights * (1.0 / jnp.sum(weights, axis=0, keepdims=True))
        dprobs = cols_dot(slot_rows(v_ref, shared, chosen), slope)
        inner = jnp.sum(probs * dprobs, axis=0, keepdims=True)
        dscores = (probs * (dprobs - inner)).astype(BF)
        dq_ref[rows, :] = (join_pair(rows_dot(dscores, keys)) * 0.125).astype(BF)
        add_rows(dk_acc, shared, chosen, plain_dot(dscores, queries))
        add_rows(dv_acc, shared, chosen, plain_dot(probs.astype(BF), slope))
        return carry

    lax.fori_loop(0, own_blocks, regular, 0, unroll=2)

    def whole(block, carry):
        @pl.when(glob_ref[block * 4] > 0)
        def _():
            rows = pl.ds(pl.multiple_of(block * BLOCK, BLOCK), BLOCK)
            first = glob_ref[block * 4 + 1]
            length = glob_ref[block * 4 + 2]
            chunks = (length + SLOTS - 1) // SLOTS
            queries = split_pair(q_ref[rows, :] * 0.125)
            slope = split_pair(c_ref[rows, :])
            slot_id = lax.broadcasted_iota(jnp.int32, (WIDE, LANES), 0) // BLOCK

            def score(step, top):
                at = pl.ds(pl.multiple_of((first + step * SLOTS) * BLOCK, BLOCK), WIDE)
                scores = cols_dot(k_ref[at, :], queries)
                scores = jnp.where(slot_id < length - step * SLOTS, scores, masked_score)
                s_ref[step] = scores
                p_ref[step] = cols_dot(v_ref[at, :], slope)
                return jnp.maximum(top, jnp.max(scores, axis=0, keepdims=True))

            top = lax.fori_loop(0, chunks, score, jnp.full((1, LANES), masked_score, F32))

            def weigh(step, kept):
                total, inner = kept
                weights = jnp.exp(s_ref[step] - top)
                s_ref[step] = weights
                return (
                    total + jnp.sum(weights, axis=0, keepdims=True),
                    inner + jnp.sum(weights * p_ref[step], axis=0, keepdims=True),
                )

            zero_row = jnp.zeros((1, LANES), F32)
            total, inner = lax.fori_loop(0, chunks, weigh, (zero_row, zero_row))
            scale = 1.0 / total
            inner = inner * scale

            def spread(step, dq_sum):
                at = pl.ds(pl.multiple_of((first + step * SLOTS) * BLOCK, BLOCK), WIDE)
                probs = s_ref[step] * scale
                dscores = (probs * (p_ref[step] - inner)).astype(BF)
                dk_acc[at, :] += plain_dot(dscores, queries)
                dv_acc[at, :] += plain_dot(probs.astype(BF), slope)
                return dq_sum + rows_dot(dscores, k_ref[at, :])

            dq_sum = lax.fori_loop(0, chunks, spread, jnp.zeros((LANES, LANES), F32))
            dq_ref[rows, :] = (join_pair(dq_sum) * 0.125).astype(BF)

        return carry

    lax.fori_loop(0, own_blocks, whole, 0)
    dk_ref[...] = dk_acc[...].astype(BF)
    dv_ref[...] = dv_acc[...].astype(BF)


def attention_calls(row_count, model_width, heads, buf_rows):
    own_blocks = row_count // BLOCK
    pairs = heads // 2
    own = lambda: pl.BlockSpec((row_count, LANES), lambda p, *_: (0, p))
    keys = lambda: pl.BlockSpec((buf_rows, LANES), lambda p, *_: (0, p))
    values = lambda: pl.BlockSpec((buf_rows, LANES), lambda p, *_: (0, p + pairs))
    params = lambda: pltpu.CompilerParams(vmem_limit_bytes=48 * 1024 * 1024)
    forward = pl.pallas_call(
        functools.partial(forward_kernel, heads, own_blocks),
        out_shape=jax.ShapeDtypeStruct((row_count, model_width), BF),
        grid_spec=pltpu.PrefetchScalarGridSpec(
            num_scalar_prefetch=3,
            grid=(pairs,),
            in_specs=[own(), keys(), values()],
            out_specs=own(),
            scratch_shapes=[pltpu.VMEM((CHUNKS, LANES, WIDE), F32)],
        ),
        compiler_params=params(),
        cost_estimate=pl.CostEstimate(
            flops=4 * row_count * WIDE * 2 * model_width, bytes_accessed=4 * buf_rows * model_width,
            transcendentals=row_count * WIDE * heads,
        ),
        name="attend_forward",
    )
    backward = pl.pallas_call(
        functools.partial(backward_kernel, heads, own_blocks),
        out_shape=(
            jax.ShapeDtypeStruct((row_count, model_width), BF),
            jax.ShapeDtypeStruct((buf_rows, model_width), BF),
            jax.ShapeDtypeStruct((buf_rows, model_width), BF),
        ),
        grid_spec=pltpu.PrefetchScalarGridSpec(
            num_scalar_prefetch=3,
            grid=(pairs,),
            in_specs=[own(), keys(), values(), own()],
            out_specs=[own(), keys(), keys()],
            scratch_shapes=[
                pltpu.VMEM((buf_rows, LANES), F32),
                pltpu.VMEM((buf_rows, LANES), F32),
                pltpu.VMEM((CHUNKS, WIDE, LANES), F32),
                pltpu.VMEM((CHUNKS, WIDE, LANES), F32),
            ],
        ),
        compiler_params=params(),
        cost_estimate=pl.CostEstimate(
            flops=10 * row_count * WIDE * 2 * model_width, bytes_accessed=8 * buf_rows * model_width,
            transcendentals=row_count * WIDE * heads,
        ),
        name="attend_backward",
    )
    return forward, backward


def on_device(
    layer_input, out_grad, doc_starts, rand_blocks, query_weight, query_bias, key_weight, value_weight,
    value_bias, output_weight, output_bias, first_gain, first_shift, inner_weight, inner_bias,
    outer_weight, outer_bias, second_gain, second_shift,
):
    row_count, model_width = layer_input.shape
    head_count = rand_blocks.shape[1]
    devices = lax.axis_size("ctx")
    own_blocks = row_count // BLOCK
    reach_shards = (REACH - 1 + own_blocks) // own_blocks
    buf_blocks = 2 * REACH + own_blocks
    own_first = lax.axis_index("ctx") * own_blocks
    buf_first = own_first - REACH
    block_total = own_blocks * devices
    own_ids = own_first + jnp.arange(own_blocks, dtype=jnp.int32)
    own_doc, own_start = doc_layout(doc_starts, own_ids)
    next_doc = doc_layout(doc_starts, own_ids + 1)[0]
    start_blocks = doc_starts // BLOCK
    later = start_blocks[None, :] > own_ids[:, None]
    doc_end = jnp.min(jnp.where(later, start_blocks[None, :], block_total), axis=1)
    glob_own = own_ids - own_start < 2

    def local(ids):
        return jnp.clip(ids - buf_first, 0, buf_blocks - 1).astype(jnp.int32)

    near = jnp.stack(
        [
            local(own_ids - 1),
            local(own_ids),
            local(own_ids + 1),
            local(own_start),
            local(own_start + 1),
            ((own_ids + 1 < block_total) & (next_doc == own_doc)).astype(jnp.int32),
            (own_ids - own_start > 2).astype(jnp.int32),
            jnp.zeros_like(own_ids),
        ],
        axis=1,
    ).reshape(-1)
    picks = local(rand_blocks).reshape(-1)
    spans = jnp.stack(
        [glob_own.astype(jnp.int32), local(own_start), doc_end - own_start, jnp.zeros_like(own_ids)], axis=1
    ).reshape(-1)
    attend, attend_back = attention_calls(row_count, model_width, head_count, buf_blocks * BLOCK)

    def gathered(value):
        return lax.all_gather(value, "ctx", axis=0, tiled=True)

    vectors = (
        query_bias, value_bias, output_bias, first_gain, first_shift, outer_bias, second_gain, second_shift, inner_bias,
    )
    w_qkv = gathered(jnp.concatenate([query_weight, key_weight, value_weight], axis=1).astype(BF))
    vector_all = gathered(jnp.concatenate(vectors).astype(BF)[None, :])
    unit = query_bias.shape[0]
    b_query, b_value, b_output, g_first, s_first, b_outer, g_second, s_second = [
        vector_all[:, i * unit : (i + 1) * unit].reshape(-1).astype(F32) for i in range(8)
    ]
    b_inner = vector_all[:, 8 * unit :].reshape(-1).astype(F32)
    w_late = gathered(jnp.concatenate([output_weight, inner_weight], axis=1).astype(BF))
    w_output, w_inner = w_late[:, :model_width], w_late[:, model_width:]
    w_outer = gathered(outer_weight.astype(BF))

    b_qkv = jnp.concatenate([b_query, jnp.zeros_like(b_query), b_value])
    qkv = (plain_dot(layer_input, w_qkv) + b_qkv).astype(BF)
    query_rows, kv_own = qkv[:, :model_width], qkv[:, model_width:]
    parts = []
    for offset in range(-reach_shards, reach_shards + 1):
        if offset == 0:
            parts.append(kv_own)
        else:
            span_rows = edge_rows(abs(offset), own_blocks)
            start_at = 0 if offset > 0 else row_count - span_rows
            parts.append(passed_along(kv_own[start_at : start_at + span_rows], "ctx", -offset))
    kv_buf = jnp.concatenate(parts, axis=0)

    context_rows = attend(near, picks, spans, query_rows, kv_buf, kv_buf)

    input_float = layer_input.astype(F32)
    resid_one = input_float + plain_dot(context_rows, w_output) + b_output
    normed_one, first_pull = jax.vjp(layer_norm, resid_one, g_first, s_first)
    normed_low = normed_one.astype(BF)
    inner_pre = plain_dot(normed_low, w_inner) + b_inner
    active_f, gelu_pull = jax.vjp(gelu_exact, inner_pre)
    active = active_f.astype(BF)
    resid_two = normed_one + plain_dot(active, w_outer) + b_outer
    normed_two, second_pull = jax.vjp(layer_norm, resid_two, g_second, s_second)
    layer_out = normed_two.astype(BF)

    def scattered(value):
        return lax.psum_scatter(value.astype(BF), "ctx", scatter_dimension=0, tiled=True).astype(F32)

    grad_two, grad_second_gain, grad_second_shift = second_pull(out_grad.astype(F32))
    grad_two_low = grad_two.astype(BF)
    grad_outer_bias = jnp.sum(grad_two_low.astype(F32), axis=0)
    grad_outer_weight = scattered(rows_dot(active, grad_two_low))
    grad_inner = gelu_pull(cols_dot(grad_two_low, w_outer))[0].astype(BF)
    grad_inner_bias = jnp.sum(grad_inner.astype(F32), axis=0)
    grad_inner_weight = scattered(rows_dot(normed_low, grad_inner))
    grad_one = grad_two + cols_dot(grad_inner, w_inner)
    grad_resid_one, grad_first_gain, grad_first_shift = first_pull(grad_one)
    grad_one_low = grad_resid_one.astype(BF)
    grad_output_bias = jnp.sum(grad_one_low.astype(F32), axis=0)
    grad_output_weight = rows_dot(context_rows, grad_one_low)
    context_gradient = cols_dot(grad_one_low, w_output).astype(BF)

    query_low, grad_key_buf, grad_value_buf = attend_back(
        near, picks, spans, query_rows, kv_buf, kv_buf, context_gradient
    )
    own_lower = REACH * BLOCK
    grad_kv_buf = jnp.concatenate([grad_key_buf, grad_value_buf], axis=1)
    kv_total = grad_kv_buf[own_lower : own_lower + row_count].astype(F32)
    lower = 0
    for offset in range(-reach_shards, reach_shards + 1):
        if offset == 0:
            lower += row_count
            continue
        span_rows = edge_rows(abs(offset), own_blocks)
        target = 0 if offset > 0 else row_count - span_rows
        got = passed_along(grad_kv_buf[lower : lower + span_rows], "ctx", offset).astype(F32)
        kv_total = kv_total + jnp.pad(got, ((target, row_count - span_rows - target), (0, 0)))
        lower += span_rows
    qkv_low = jnp.concatenate([query_low, kv_total.astype(BF)], axis=1)
    grad_qkv_weight = rows_dot(layer_input, qkv_low)
    grad_qkv_bias = jnp.sum(qkv_low.astype(F32), axis=0)
    grad_input = grad_resid_one + cols_dot(qkv_low, w_qkv)
    attn_grads = scattered(jnp.concatenate([grad_qkv_weight, grad_output_weight], axis=1))
    vector_grads = jnp.concatenate(
        [
            value.reshape(devices, -1)
            for value in (
                grad_qkv_bias[:model_width], grad_qkv_bias[2 * model_width :], grad_output_bias, grad_first_gain,
                grad_first_shift, grad_outer_bias, grad_second_gain, grad_second_shift, grad_inner_bias,
            )
        ],
        axis=1,
    )
    vector_sums = lax.psum_scatter(vector_grads, "ctx", scatter_dimension=0, tiled=True)[0]
    v_query, v_value, v_output, v_gain1, v_shift1, v_outer, v_gain2, v_shift2 = [
        vector_sums[i * unit : (i + 1) * unit] for i in range(8)
    ]
    v_inner = vector_sums[8 * unit :]
    m = model_width
    return (
        layer_out, grad_input, attn_grads[:, :m], v_query, attn_grads[:, m : 2 * m], attn_grads[:, 2 * m : 3 * m],
        v_value, attn_grads[:, 3 * m :], v_output, v_gain1, v_shift1, grad_inner_weight, v_inner,
        grad_outer_weight, v_outer, v_gain2, v_shift2,
    )


def solution(mesh):
    rows, line = P("ctx", None), P("ctx")
    in_specs = (
        rows, rows, P(), P("ctx", None, None), rows, line, rows, rows, line, rows, line, line, line, rows, line, rows,
        line, line, line,
    )
    out_specs = (
        rows, rows, rows, line, rows, rows, line, rows, line, line, line, rows, line, rows, line, line, line,
    )
    return jax.shard_map(on_device, mesh=mesh, in_specs=in_specs, out_specs=out_specs, check_vma=False)
```

```python
import functools
import math

import jax
import jax.numpy as jnp
from jax import lax
from jax.experimental import pallas as pl
from jax.experimental.pallas import tpu as pltpu
from jax.sharding import PartitionSpec as P

BLOCK = 64
DOC_MAX = 32
REACH = DOC_MAX - 1
SLOTS = 8
WIDE = SLOTS * BLOCK
CHUNKS = DOC_MAX // SLOTS
LANES = 128

norm_eps = 1e-06
masked_score = -1e30
BF = jnp.bfloat16
F32 = jnp.float32


def layer_norm(hidden, scale_gain, shift_vec):
    row_mean = jnp.mean(hidden, axis=-1, keepdims=True)
    centred = hidden - row_mean
    variance = jnp.mean(centred * centred, axis=-1, keepdims=True)
    return centred * lax.rsqrt(variance + norm_eps) * scale_gain + shift_vec


def gelu_exact(inner_pre):
    return jax.nn.gelu(inner_pre, approximate=False)


def plain_dot(left, right):
    return jnp.dot(left, right, preferred_element_type=F32)


def rows_dot(left, right):
    return lax.dot_general(left, right, (((0,), (0,)), ((), ())), preferred_element_type=F32)


def cols_dot(left, right):
    return lax.dot_general(left, right, (((1,), (1,)), ((), ())), preferred_element_type=F32)


def doc_layout(doc_starts, block_ids):
    start_blocks = doc_starts // BLOCK
    before = start_blocks[None, :] <= block_ids[:, None]
    doc_ids = jnp.sum(before.astype(jnp.int32), axis=1) - 1
    first_block = jnp.max(jnp.where(before, start_blocks[None, :], -1), axis=1)
    return (doc_ids, first_block)


def link_orders(count):
    bits = count.bit_length() - 1
    assert count == 1 << bits and bits >= 4, count
    high = list(range(bits - 1, 2, -1))
    return [[1] + high + [2, 0], [1, 2] + high + [0], [1] + high[:-1] + [2] + high[-1:] + [0]]


def bit_of(index, bit):
    return (index // (1 << bit)) % 2


def across(index, bit):
    return index + (1 << bit) * (1 - 2 * bit_of(index, bit))


def place_of(index, order):
    return sum(bit_of(index, bit) * (1 << k) for k, bit in enumerate(order))


def remote(source, target, send_sem, recv_sem, device):
    return pltpu.make_async_remote_copy(
        src_ref=source, dst_ref=target, send_sem=send_sem, recv_sem=recv_sem, device_id=(device,),
        device_id_type=pl.DeviceIdType.MESH,
    )


def halo_sizes(own_rows):
    far = REACH * BLOCK - 2 * own_rows
    assert 0 < far <= own_rows, own_rows
    return far, [0] + [far + own_rows * i for i in range(6)]


def halo_links(me, count):
    odd = me % 2
    partner = me - 3 + 6 * odd
    return odd, me >= 2, me < count - 2, (partner >= 0) & (partner < count), partner


def greet(me, bits, count):
    barrier = pltpu.get_barrier_semaphore()

    def hello(device):
        pl.semaphore_signal(barrier, inc=1, device_id=(device,), device_id_type=pl.DeviceIdType.MESH)

    _, has_before, has_after, has_far, partner = halo_links(me, count)
    for bit in range(bits):
        hello(across(me, bit))

    @pl.when(has_before)
    def _():
        hello(me - 2)

    @pl.when(has_after)
    def _():
        hello(me + 2)

    @pl.when(has_far)
    def _():
        hello(partner)

    expected = bits + has_before.astype(jnp.int32) + has_after.astype(jnp.int32) + has_far.astype(jnp.int32)
    pl.semaphore_wait(barrier, expected)


def gather_kernel(
    count, wq_ref, wk_ref, wv_ref, v_ref, x_ref, w_out, v_out, x_out, low_w, low_v, buf_a, buf_b, buf_c, buf_v, zeros, local_sem, out_sem, send_sem,
    recv_sem, halo_send, halo_recv, fill_sem,
):
    me = lax.axis_index("ctx")
    orders = link_orders(count)
    bits = len(orders[0])
    width = wq_ref.shape[1]
    low_w[:, :width] = wq_ref[...].astype(BF)
    for i in range(width // LANES):
        start = width + 2 * i * LANES
        low_w[:, start : start + LANES] = wk_ref[:, i * LANES : (i + 1) * LANES].astype(BF)
        low_w[:, start + LANES : start + 2 * LANES] = wv_ref[:, i * LANES : (i + 1) * LANES].astype(BF)
    low_v[...] = v_ref[...].astype(BF)
    orders = orders + [orders[0]]
    bufs = [buf_a, buf_b, buf_c, buf_v]
    sources = [low_w.at[:, pl.ds(i * width, width)] for i in range(3)] + [low_v]
    places = [place_of(me, order) for order in orders]
    full = x_ref.shape[0]
    part, piece = halo_sizes(full)
    odd, has_before, has_after, has_far, partner = halo_links(me, count)
    sibling = across(me, 0)

    def rows(start, size):
        return x_out.at[pl.ds(pl.multiple_of(start, BLOCK), size), :]

    def halo(index, source, target, device):
        return remote(source, target, halo_send.at[index], halo_recv.at[index], device)

    zeros[...] = jnp.zeros_like(zeros)
    keep_own = pltpu.make_async_copy(x_ref, rows(piece[3], full), local_sem.at[4])
    keep_own.start()
    greet(me, bits, count)
    for i in range(4):
        pltpu.make_async_copy(sources[i], bufs[i].at[places[i]], local_sem.at[i]).start()

    after = halo(0, x_ref, rows(piece[1], full), me + 2)
    before = halo(1, x_ref, rows(piece[5], full), me - 2)
    far_rows = x_ref.at[pl.ds(pl.multiple_of(odd * (full - part), BLOCK), part), :]
    far = halo(2, far_rows, rows((1 - odd) * piece[6], part), partner)
    own = halo(3, x_ref, rows(piece[2] + odd * (piece[4] - piece[2]), full), sibling)
    wide = halo(
        4, rows(piece[5] + odd * (piece[1] - piece[5]), full), rows(piece[4] + odd * (piece[2] - piece[4]), full), sibling
    )
    edge_from = (piece[1] + full - part) * (1 - odd) + piece[5] * odd
    edge = halo(5, rows(edge_from, part), rows(piece[6] * odd, part), sibling)
    has_wide = jnp.where(odd == 1, has_before, has_after)
    has_edge = jnp.where(odd == 1, has_after, has_before)

    for i in range(4):
        pltpu.make_async_copy(sources[i], bufs[i].at[places[i]], local_sem.at[i]).wait()
    copies = [own]
    for k in range(bits):
        stage = []
        for i in range(4):
            held = bufs[i].at[pl.ds((places[i] // (1 << k)) * (1 << k), 1 << k)]
            copy = remote(held, held, send_sem.at[i, k], recv_sem.at[i, k], across(me, orders[i][k]))
            copy.start()
            stage.append(copy)
        for copy in stage:
            copy.wait_recv()
        copies += stage
        if k == 0:
            own.start()
            pl.when(has_after)(after.start)
            pl.when(has_before)(before.start)
            pl.when(has_far)(far.start)

    def put(j, carry):
        for i in range(3):
            pltpu.make_async_copy(
                bufs[i].at[place_of(j, orders[i])], w_out.at[j, :, pl.ds(i * width, width)], out_sem.at[i]
            ).start()
        pltpu.make_async_copy(buf_v.at[place_of(j, orders[3])], v_out.at[j], out_sem.at[3]).start()
        return carry

    lax.fori_loop(0, count, put, 0)

    @pl.when(has_before)
    def _():
        halo(0, x_ref, rows(piece[1], full), sibling).wait_recv()

    @pl.when(has_after)
    def _():
        halo(1, x_ref, rows(piece[5], full), sibling).wait_recv()

    @pl.when(has_wide)
    def _():
        wide.start()

    @pl.when(has_edge)
    def _():
        edge.start()

    def fill(missing, start, size):
        @pl.when(missing)
        def _():
            copy = pltpu.make_async_copy(zeros.at[pl.ds(0, size), :], rows(start, size), fill_sem.at[0])
            copy.start()
            copy.wait()

    fill(jnp.logical_not(has_before), piece[1], full)
    fill(jnp.logical_not(has_after), piece[5], full)
    gets_wide = jnp.where(odd == 1, has_after, has_before)
    gets_edge = jnp.where(odd == 1, has_before, has_after)
    wide_at = piece[2] + odd * (piece[4] - piece[2])
    edge_at = piece[6] * (1 - odd)
    far_at = piece[6] * odd
    own_at = piece[4] + odd * (piece[2] - piece[4])
    fill(jnp.logical_not(gets_wide), wide_at, full)
    fill(jnp.logical_not(gets_edge), edge_at, part)
    fill(jnp.logical_not(has_far), far_at, part)
    halo(3, x_ref, rows(own_at, full), sibling).wait_recv()

    @pl.when(has_far)
    def _():
        halo(2, far_rows, rows(far_at, part), sibling).wait_recv()

    @pl.when(gets_wide)
    def _():
        halo(4, x_ref, rows(wide_at, full), sibling).wait_recv()

    @pl.when(gets_edge)
    def _():
        halo(5, far_rows, rows(edge_at, part), sibling).wait_recv()

    for copy in copies:
        copy.wait_send()
    for exists, copy in ((has_after, after), (has_before, before), (has_far, far), (has_wide, wide), (has_edge, edge)):
        pl.when(exists)(copy.wait_send)
    keep_own.wait()
    for i in range(3):
        pltpu.make_async_copy(bufs[i], w_out.at[:, :, pl.ds(i * width, width)], out_sem.at[i]).wait()
    pltpu.make_async_copy(buf_v, v_out, out_sem.at[3]).wait()


def gather_weights(query, key, value, vectors, own, count):
    rows, columns = query.shape[0], 3 * query.shape[1]
    bits = count.bit_length() - 1
    vmem, any_space = pl.BlockSpec(memory_space=pltpu.VMEM), pl.BlockSpec(memory_space=pl.ANY)
    return pl.pallas_call(
        functools.partial(gather_kernel, count),
        out_shape=(
            jax.ShapeDtypeStruct((count, rows, columns), BF),
            jax.ShapeDtypeStruct((count,) + vectors.shape, BF),
            jax.ShapeDtypeStruct((own.shape[0] + 2 * REACH * BLOCK, own.shape[1]), BF),
        ),
        in_specs=[vmem] * 5,
        out_specs=[any_space, any_space, any_space],
        scratch_shapes=[pltpu.VMEM((rows, columns), BF), pltpu.VMEM(vectors.shape, BF)]
        + [pltpu.VMEM((count, rows, columns // 3), BF)] * 3
        + [
            pltpu.VMEM((count,) + vectors.shape, BF),
            pltpu.VMEM(own.shape, BF),
            pltpu.SemaphoreType.DMA((5,)),
            pltpu.SemaphoreType.DMA((4,)),
            pltpu.SemaphoreType.DMA((4, bits)),
            pltpu.SemaphoreType.DMA((4, bits)),
            pltpu.SemaphoreType.DMA((6,)),
            pltpu.SemaphoreType.DMA((6,)),
            pltpu.SemaphoreType.DMA((1,)),
        ],
        compiler_params=pltpu.CompilerParams(
            collective_id=0, has_side_effects=True, vmem_limit_bytes=60 * 1024 * 1024
        ),
        cost_estimate=pl.CostEstimate(flops=0, bytes_accessed=200_000_000, transcendentals=0),
        name="gather_weights",
    )(query, key, value, vectors, own)


def reduce_kernel(
    count, q_ref, kv_ref, v_ref, x_ref, wq_out, wk_out, wv_out, v_out, x_out, buf_a, buf_b, buf_c, got_a, got_b, got_c, sum_v, got_v,
    left, mid, right, e_own, e_wide, e_edge, e_far, from_after, from_before, load_sem, send_sem, recv_sem, halo_send,
    halo_recv,
):
    me = lax.axis_index("ctx")
    orders = link_orders(count)
    bits = len(orders[0])
    bufs, gots = [buf_a, buf_b, buf_c], [got_a, got_b, got_c]
    width = q_ref.shape[2]
    full = left.shape[0]
    part, piece = halo_sizes(full)
    odd, has_before, has_after, has_far, partner = halo_links(me, count)
    sibling = across(me, 0)

    def rows(start, size):
        return x_ref.at[pl.ds(pl.multiple_of(start, BLOCK), size), :]

    def halo(index, source, target, device):
        return remote(source, target, halo_send.at[index], halo_recv.at[index], device)

    loads = [
        pltpu.make_async_copy(rows(piece[1], full), left, load_sem.at[4]),
        pltpu.make_async_copy(rows(piece[3], full), mid, load_sem.at[5]),
        pltpu.make_async_copy(rows(piece[5], full), right, load_sem.at[6]),
    ]
    for copy in loads:
        copy.start()

    def load(j, carry):
        pltpu.make_async_copy(q_ref.at[j], bufs[0].at[place_of(j, orders[0])], load_sem.at[0]).start()
        for i in (1, 2):
            pltpu.make_async_copy(
                kv_ref.at[j, :, pl.ds((i - 1) * width, width)], bufs[i].at[place_of(j, orders[i])], load_sem.at[i]
            ).start()
        return carry

    lax.fori_loop(0, count, load, 0)
    first_sum = pltpu.make_async_copy(v_ref, sum_v.at[0], load_sem.at[3])
    first_sum.start()
    greet(me, bits, count)

    swaps = [
        halo(3, rows(piece[2] + odd * (piece[4] - piece[2]), full), e_wide, sibling),
        halo(4, rows(piece[6] * (1 - odd), part), e_edge, sibling),
        halo(5, rows(piece[4] + odd * (piece[2] - piece[4]), full), e_own, sibling),
    ]
    for copy in swaps:
        copy.start()
    far = halo(2, rows(piece[6] * odd, part), e_far, partner)

    @pl.when(has_far)
    def _():
        far.start()

    for copy in loads:
        copy.wait()
    swaps[0].wait_recv()
    swaps[1].wait_recv()

    def add_into(target, start, source, size):
        def add(j, carry):
            at = pl.ds(pl.multiple_of(start + j * BLOCK, BLOCK), BLOCK)
            total = target[at, :].astype(F32) + source[pl.ds(pl.multiple_of(j * BLOCK, BLOCK), BLOCK), :].astype(F32)
            target[at, :] = total.astype(target.dtype)
            return carry

        lax.fori_loop(0, size // BLOCK, add, 0)

    @pl.when(odd == 0)
    def _():
        add_into(left, full - part, e_edge, part)
        add_into(right, 0, e_wide, full)

    @pl.when(odd == 1)
    def _():
        add_into(left, 0, e_wide, full)
        add_into(right, 0, e_edge, part)

    before = halo(0, left, from_after, me - 2)
    after = halo(1, right, from_before, me + 2)

    @pl.when(has_before)
    def _():
        before.start()

    @pl.when(has_after)
    def _():
        after.start()

    for i in range(3):
        source = q_ref if i == 0 else kv_ref.at[:, :, pl.ds((i - 1) * width, width)]
        pltpu.make_async_copy(source, bufs[i], load_sem.at[i]).wait()
    first_sum.wait()
    places = [place_of(me, order) for order in orders]
    copies = []
    for k in range(bits):
        bit = bits - 1 - k
        half = 1 << bit
        offset = count - 2 * half
        stage = []
        for i in range(3):
            keep = (places[i] // half) * half
            give = keep + half * (1 - 2 * bit_of(places[i], bit))
            copy = remote(
                bufs[i].at[pl.ds(give, half)], gots[i].at[pl.ds(offset, half)], send_sem.at[i, k], recv_sem.at[i, k],
                across(me, orders[i][bit]),
            )
            copy.start()
            stage.append(copy)
        copy = remote(sum_v.at[k], got_v.at[k], send_sem.at[3, k], recv_sem.at[3, k], across(me, orders[0][bit]))
        copy.start()
        stage.append(copy)
        for i in range(3):
            stage[i].wait_recv()
            keep = (places[i] // half) * half
            if k == bits - 1:
                total = bufs[i][keep].astype(F32) + gots[i][offset].astype(F32)
                if i == 0:
                    wq_out[...] = total
                else:
                    for j in range(width // LANES):
                        place = ((i - 1) * width // LANES + j) // 2 * LANES
                        target = wv_out if ((i - 1) * width // LANES + j) % 2 else wk_out
                        target[:, place : place + LANES] = total[:, j * LANES : (j + 1) * LANES]
            else:

                def add(j, carry, i=i, keep=keep, offset=offset):
                    total = bufs[i][keep + j].astype(F32) + gots[i][offset + j].astype(F32)
                    bufs[i][keep + j] = total.astype(BF)
                    return carry

                lax.fori_loop(0, half, add, 0)
        stage[3].wait_recv()
        if k == bits - 1:
            v_out[...] = sum_v[k] + got_v[k]
        else:
            sum_v[k + 1] = sum_v[k] + got_v[k]
        copies += stage

    swaps[2].wait_recv()

    def start_sum(j, carry):
        at = pl.ds(pl.multiple_of(j * BLOCK, BLOCK), BLOCK)
        x_out[at, :] = mid[at, :].astype(F32) + e_own[at, :].astype(F32)
        return carry

    lax.fori_loop(0, full // BLOCK, start_sum, 0)

    @pl.when(has_far)
    def _():
        far.wait_recv()
        add_into(x_out, odd * (full - part), e_far, part)

    @pl.when(has_after)
    def _():
        before.wait_recv()
        add_into(x_out, 0, from_after, full)

    @pl.when(has_before)
    def _():
        after.wait_recv()
        add_into(x_out, 0, from_before, full)

    for copy in copies + swaps:
        copy.wait_send()
    for exists, copy in ((has_after, after), (has_before, before), (has_far, far)):
        pl.when(exists)(copy.wait_send)


def reduce_grads(query_grads, kv_grads, vectors, halo_grads, own_rows, count):
    _, rows, columns = query_grads.shape
    bits = count.bit_length() - 1
    vmem, any_space = pl.BlockSpec(memory_space=pltpu.VMEM), pl.BlockSpec(memory_space=pl.ANY)
    slabs = pltpu.VMEM((count, rows, columns), BF)
    stages = pltpu.VMEM((bits,) + vectors.shape, F32)
    part, _ = halo_sizes(own_rows)
    whole, piece = pltpu.VMEM((own_rows, columns), BF), pltpu.VMEM((part, columns), BF)
    return pl.pallas_call(
        functools.partial(reduce_kernel, count),
        out_shape=(
            jax.ShapeDtypeStruct((rows, columns), F32),
            jax.ShapeDtypeStruct((rows, columns), F32),
            jax.ShapeDtypeStruct((rows, columns), F32),
            jax.ShapeDtypeStruct(vectors.shape, F32),
            jax.ShapeDtypeStruct((own_rows, columns), F32),
        ),
        in_specs=[any_space, any_space, vmem, any_space],
        out_specs=[vmem] * 5,
        scratch_shapes=[slabs] * 6
        + [stages, stages, whole, whole, whole, whole, whole, piece, piece, whole, whole]
        + [
            pltpu.SemaphoreType.DMA((7,)),
            pltpu.SemaphoreType.DMA((4, bits)),
            pltpu.SemaphoreType.DMA((4, bits)),
            pltpu.SemaphoreType.DMA((6,)),
            pltpu.SemaphoreType.DMA((6,)),
        ],
        compiler_params=pltpu.CompilerParams(
            collective_id=1, has_side_effects=True, vmem_limit_bytes=60 * 1024 * 1024
        ),
        cost_estimate=pl.CostEstimate(flops=0, bytes_accessed=200_000_000, transcendentals=0),
        name="reduce_grads",
    )(query_grads, kv_grads, vectors, halo_grads)


def low_half():
    return lax.broadcasted_iota(jnp.int32, (BLOCK, LANES), 1) < LANES // 2


def split_pair(rows):
    half = low_half()
    zero = jnp.zeros_like(rows)
    return jnp.concatenate([jnp.where(half, rows, zero), jnp.where(half, zero, rows)], axis=0)


def join_pair(rows):
    return jnp.where(low_half(), rows[:BLOCK], rows[BLOCK:])


KEY, VALUE = slice(0, LANES), slice(LANES, 2 * LANES)


def block_at(ref, position, side):
    return ref[pl.ds(pl.multiple_of(position * BLOCK, BLOCK), BLOCK), side]


def slots_of(near_ref, rand_ref, block, pair, heads):
    shared = [near_ref[block * 8 + i] for i in range(5)]
    at = (block * heads + 2 * pair) * 3
    chosen = [(rand_ref[at + i], rand_ref[at + 3 + i]) for i in range(3)]
    return shared, chosen


def slot_rows(ref, side, shared, chosen):
    half = low_half()
    parts = [block_at(ref, i, side) for i in shared]
    parts += [jnp.where(half, block_at(ref, a, side), block_at(ref, b, side)) for a, b in chosen]
    return jnp.concatenate(parts, axis=0)


def slot_bias(near_ref, block):
    after = jnp.where(near_ref[block * 8 + 5] > 0, 0.0, masked_score).astype(F32)
    lead = jnp.where(near_ref[block * 8 + 6] > 0, 0.0, masked_score).astype(F32)
    return after, lead


def forward_kernel(heads, own_blocks, near_ref, rand_ref, glob_ref, q_ref, kv_ref, o_ref, s_ref):
    pair = pl.program_id(0)
    slot_id = lax.broadcasted_iota(jnp.int32, (1, WIDE), 1) // BLOCK

    def regular(block, carry):
        rows = pl.ds(pl.multiple_of(block * BLOCK, BLOCK), BLOCK)
        shared, chosen = slots_of(near_ref, rand_ref, block, pair, heads)
        queries = split_pair(q_ref[rows, :] * 0.125)
        scores = cols_dot(queries, slot_rows(kv_ref, KEY, shared, chosen))
        after, lead = slot_bias(near_ref, block)
        scores = scores + jnp.where(slot_id == 2, after, jnp.where(slot_id == 4, lead, 0.0))
        weights = jnp.exp(scores - jnp.max(scores, axis=1, keepdims=True))
        probs = weights * (1.0 / jnp.sum(weights, axis=1, keepdims=True))
        mixed = plain_dot(probs.astype(BF), slot_rows(kv_ref, VALUE, shared, chosen))
        o_ref[rows, :] = join_pair(mixed).astype(BF)
        return carry

    lax.fori_loop(0, own_blocks, regular, 0, unroll=4)

    def whole(block, carry):
        @pl.when(glob_ref[block * 4] > 0)
        def _():
            rows = pl.ds(pl.multiple_of(block * BLOCK, BLOCK), BLOCK)
            first = glob_ref[block * 4 + 1]
            length = glob_ref[block * 4 + 2]
            chunks = (length + SLOTS - 1) // SLOTS
            queries = split_pair(q_ref[rows, :] * 0.125)

            def score(step, top):
                at = pl.ds(pl.multiple_of((first + step * SLOTS) * BLOCK, BLOCK), WIDE)
                scores = cols_dot(queries, kv_ref[at, KEY])
                scores = jnp.where(slot_id < length - step * SLOTS, scores, masked_score)
                s_ref[step] = scores
                return jnp.maximum(top, jnp.max(scores, axis=1, keepdims=True))

            top = lax.fori_loop(0, chunks, score, jnp.full((LANES, 1), masked_score, F32))

            def mix(step, kept):
                total, acc = kept
                at = pl.ds(pl.multiple_of((first + step * SLOTS) * BLOCK, BLOCK), WIDE)
                weights = jnp.exp(s_ref[step] - top)
                return (
                    total + jnp.sum(weights, axis=1, keepdims=True),
                    acc + plain_dot(weights.astype(BF), kv_ref[at, VALUE]),
                )

            total, acc = lax.fori_loop(
                0, chunks, mix, (jnp.zeros((LANES, 1), F32), jnp.zeros((LANES, LANES), F32))
            )
            o_ref[rows, :] = join_pair(acc * (1.0 / total)).astype(BF)

        return carry

    lax.fori_loop(0, own_blocks, whole, 0)


def backward_kernel(
    heads, own_blocks, near_ref, rand_ref, glob_ref, q_ref, kv_ref, c_ref,
    dq_ref, dkv_ref, sum_ref, dk_acc, dv_acc, s_ref, p_ref,
):
    pair = pl.program_id(0)
    dk_acc[...] = jnp.zeros_like(dk_acc)
    dv_acc[...] = jnp.zeros_like(dv_acc)
    half = low_half()

    def add_rows(acc, shared, chosen, update):
        for i, position in enumerate(shared):
            at = pl.ds(pl.multiple_of(position * BLOCK, BLOCK), BLOCK)
            acc[at, :] += update[i * BLOCK : (i + 1) * BLOCK]
        for i, (one, two) in enumerate(chosen):
            piece = update[(5 + i) * BLOCK : (6 + i) * BLOCK]
            at = pl.ds(pl.multiple_of(one * BLOCK, BLOCK), BLOCK)
            acc[at, :] += jnp.where(half, piece, 0.0)
            at = pl.ds(pl.multiple_of(two * BLOCK, BLOCK), BLOCK)
            acc[at, :] += jnp.where(half, 0.0, piece)

    def regular(block, carry):
        rows = pl.ds(pl.multiple_of(block * BLOCK, BLOCK), BLOCK)
        shared, chosen = slots_of(near_ref, rand_ref, block, pair, heads)
        queries = split_pair(q_ref[rows, :] * 0.125)
        slope = c_ref[rows, :]
        slope = split_pair(jnp.where(glob_ref[block * 4] > 0, jnp.zeros_like(slope), slope))
        keys = slot_rows(kv_ref, KEY, shared, chosen)
        scores = cols_dot(keys, queries)
        after, lead = slot_bias(near_ref, block)
        scores = jnp.concatenate(
            [
                scores[: 2 * BLOCK],
                scores[2 * BLOCK : 3 * BLOCK] + after,
                scores[3 * BLOCK : 4 * BLOCK],
                scores[4 * BLOCK : 5 * BLOCK] + lead,
                scores[5 * BLOCK :],
            ],
            axis=0,
        )
        weights = jnp.exp(scores - jnp.max(scores, axis=0, keepdims=True))
        probs = weights * (1.0 / jnp.sum(weights, axis=0, keepdims=True))
        dprobs = cols_dot(slot_rows(kv_ref, VALUE, shared, chosen), slope)
        inner = jnp.sum(probs * dprobs, axis=0, keepdims=True)
        dscores = (probs * (dprobs - inner)).astype(BF)
        dq_ref[rows, :] = (join_pair(rows_dot(dscores, keys)) * 0.125).astype(BF)
        add_rows(dk_acc, shared, chosen, plain_dot(dscores, queries))
        add_rows(dv_acc, shared, chosen, plain_dot(probs.astype(BF), slope))
        return carry

    lax.fori_loop(0, own_blocks, regular, 0, unroll=2)

    def whole(block, carry):
        @pl.when(glob_ref[block * 4] > 0)
        def _():
            rows = pl.ds(pl.multiple_of(block * BLOCK, BLOCK), BLOCK)
            first = glob_ref[block * 4 + 1]
            length = glob_ref[block * 4 + 2]
            chunks = (length + SLOTS - 1) // SLOTS
            queries = split_pair(q_ref[rows, :] * 0.125)
            slope = split_pair(c_ref[rows, :])
            slot_id = lax.broadcasted_iota(jnp.int32, (WIDE, LANES), 0) // BLOCK

            def score(step, top):
                at = pl.ds(pl.multiple_of((first + step * SLOTS) * BLOCK, BLOCK), WIDE)
                scores = cols_dot(kv_ref[at, KEY], queries)
                scores = jnp.where(slot_id < length - step * SLOTS, scores, masked_score)
                s_ref[step] = scores
                p_ref[step] = cols_dot(kv_ref[at, VALUE], slope)
                return jnp.maximum(top, jnp.max(scores, axis=0, keepdims=True))

            top = lax.fori_loop(0, chunks, score, jnp.full((1, LANES), masked_score, F32))

            def weigh(step, kept):
                total, inner = kept
                weights = jnp.exp(s_ref[step] - top)
                s_ref[step] = weights
                return (
                    total + jnp.sum(weights, axis=0, keepdims=True),
                    inner + jnp.sum(weights * p_ref[step], axis=0, keepdims=True),
                )

            zero_row = jnp.zeros((1, LANES), F32)
            total, inner = lax.fori_loop(0, chunks, weigh, (zero_row, zero_row))
            scale = 1.0 / total
            inner = inner * scale

            def spread(step, dq_sum):
                at = pl.ds(pl.multiple_of((first + step * SLOTS) * BLOCK, BLOCK), WIDE)
                probs = s_ref[step] * scale
                dscores = (probs * (p_ref[step] - inner)).astype(BF)
                dk_acc[at, :] += plain_dot(dscores, queries)
                dv_acc[at, :] += plain_dot(probs.astype(BF), slope)
                return dq_sum + rows_dot(dscores, kv_ref[at, KEY])

            dq_sum = lax.fori_loop(0, chunks, spread, jnp.zeros((LANES, LANES), F32))
            dq_ref[rows, :] = (join_pair(dq_sum) * 0.125).astype(BF)

        return carry

    lax.fori_loop(0, own_blocks, whole, 0)
    dkv_ref[:, KEY] = dk_acc[...].astype(BF)
    dv_low = dv_acc[...].astype(BF)
    dkv_ref[:, VALUE] = dv_low
    sum_ref[0:1, :] = jnp.sum(dq_ref[...].astype(F32), axis=0, keepdims=True)
    sum_ref[1:2, :] = jnp.sum(dv_low.astype(F32), axis=0, keepdims=True)


def attention_calls(row_count, model_width, heads, buf_rows):
    own_blocks = row_count // BLOCK
    pairs = heads // 2
    own = lambda: pl.BlockSpec((row_count, LANES), lambda p, *_: (0, p))
    both = lambda: pl.BlockSpec((buf_rows, 2 * LANES), lambda p, *_: (0, p))
    params = lambda: pltpu.CompilerParams(vmem_limit_bytes=48 * 1024 * 1024)
    forward = pl.pallas_call(
        functools.partial(forward_kernel, heads, own_blocks),
        out_shape=jax.ShapeDtypeStruct((row_count, model_width), BF),
        grid_spec=pltpu.PrefetchScalarGridSpec(
            num_scalar_prefetch=3,
            grid=(pairs,),
            in_specs=[own(), both()],
            out_specs=own(),
            scratch_shapes=[pltpu.VMEM((CHUNKS, LANES, WIDE), F32)],
        ),
        compiler_params=params(),
        cost_estimate=pl.CostEstimate(
            flops=4 * row_count * WIDE * 2 * model_width, bytes_accessed=4 * buf_rows * model_width,
            transcendentals=row_count * WIDE * heads,
        ),
        name="attend_forward",
    )
    backward = pl.pallas_call(
        functools.partial(backward_kernel, heads, own_blocks),
        out_shape=(
            jax.ShapeDtypeStruct((row_count, model_width), BF),
            jax.ShapeDtypeStruct((buf_rows, 2 * model_width), BF),
            jax.ShapeDtypeStruct((2, model_width), F32),
        ),
        grid_spec=pltpu.PrefetchScalarGridSpec(
            num_scalar_prefetch=3,
            grid=(pairs,),
            in_specs=[own(), both(), own()],
            out_specs=[own(), both(), pl.BlockSpec((2, LANES), lambda p, *_: (0, p))],
            scratch_shapes=[
                pltpu.VMEM((buf_rows, LANES), F32),
                pltpu.VMEM((buf_rows, LANES), F32),
                pltpu.VMEM((CHUNKS, WIDE, LANES), F32),
                pltpu.VMEM((CHUNKS, WIDE, LANES), F32),
            ],
        ),
        compiler_params=params(),
        cost_estimate=pl.CostEstimate(
            flops=10 * row_count * WIDE * 2 * model_width, bytes_accessed=8 * buf_rows * model_width,
            transcendentals=row_count * WIDE * heads,
        ),
        name="attend_backward",
    )
    return forward, backward


def interleaved(one, two):
    return jnp.concatenate(
        [side[..., i : i + LANES] for i in range(0, one.shape[-1], LANES) for side in (one, two)], axis=-1
    )


def on_device(
    layer_input, out_grad, doc_starts, rand_blocks, query_weight, query_bias, key_weight, value_weight,
    value_bias, output_weight, output_bias, first_gain, first_shift, inner_weight, inner_bias,
    outer_weight, outer_bias, second_gain, second_shift,
):
    row_count, model_width = layer_input.shape
    head_count = rand_blocks.shape[1]
    devices = lax.axis_size("ctx")
    own_blocks = row_count // BLOCK
    buf_blocks = 2 * REACH + own_blocks
    own_first = lax.axis_index("ctx") * own_blocks
    buf_first = own_first - REACH
    block_total = own_blocks * devices
    own_ids = own_first + jnp.arange(own_blocks, dtype=jnp.int32)
    own_doc, own_start = doc_layout(doc_starts, own_ids)
    next_doc = doc_layout(doc_starts, own_ids + 1)[0]
    start_blocks = doc_starts // BLOCK
    later = start_blocks[None, :] > own_ids[:, None]
    doc_end = jnp.min(jnp.where(later, start_blocks[None, :], block_total), axis=1)
    glob_own = own_ids - own_start < 2

    def local(ids):
        return jnp.clip(ids - buf_first, 0, buf_blocks - 1).astype(jnp.int32)

    near = jnp.stack(
        [
            local(own_ids - 1),
            local(own_ids),
            local(own_ids + 1),
            local(own_start),
            local(own_start + 1),
            ((own_ids + 1 < block_total) & (next_doc == own_doc)).astype(jnp.int32),
            (own_ids - own_start > 2).astype(jnp.int32),
            jnp.zeros_like(own_ids),
        ],
        axis=1,
    ).reshape(-1)
    picks = local(rand_blocks).reshape(-1)
    spans = jnp.stack(
        [glob_own.astype(jnp.int32), local(own_start), doc_end - own_start, jnp.zeros_like(own_ids)], axis=1
    ).reshape(-1)
    attend, attend_back = attention_calls(row_count, model_width, head_count, buf_blocks * BLOCK)
    m = model_width
    unit = query_bias.shape[0]
    weight_rows = query_weight.shape[0]

    def gathered(value):
        return lax.all_gather(value, "ctx", axis=0, tiled=True)

    vectors = jnp.concatenate(
        [
            query_bias, value_bias, output_bias, first_gain, first_shift, outer_bias, second_gain, second_shift,
            inner_bias,
        ]
    )
    lane_pad = -vectors.shape[0] % LANES
    first_all, vector_all, x_buf = gather_weights(
        query_weight, key_weight, value_weight, jnp.pad(vectors, (0, lane_pad))[None, :], layer_input, devices
    )
    w_qkv = first_all.reshape(m, 3 * m)
    vector_all = vector_all[:, 0].astype(F32)
    b_query, b_value, b_output, g_first, s_first, b_outer, g_second, s_second = [
        vector_all[:, i * unit : (i + 1) * unit].reshape(-1) for i in range(8)
    ]
    b_inner = vector_all[:, 8 * unit : 8 * unit + inner_bias.shape[0]].reshape(-1)
    w_late = gathered(jnp.concatenate([output_weight, inner_weight], axis=1).astype(BF))
    w_output, w_inner = w_late[:, :m], w_late[:, m:]
    w_outer = gathered(outer_weight.astype(BF))
    w_query, w_kv = w_qkv[:, :m], w_qkv[:, m:]

    query_rows = (plain_dot(layer_input, w_query) + b_query).astype(BF)
    kv_buf = (plain_dot(x_buf, w_kv) + interleaved(jnp.zeros_like(b_value), b_value)).astype(BF)
    context_rows = attend(near, picks, spans, query_rows, kv_buf)

    input_float = layer_input.astype(F32)
    resid_one = input_float + plain_dot(context_rows, w_output) + b_output
    normed_one, first_pull = jax.vjp(layer_norm, resid_one, g_first, s_first)
    normed_low = normed_one.astype(BF)
    inner_pre = plain_dot(normed_low, w_inner) + b_inner
    active_f, gelu_pull = jax.vjp(gelu_exact, inner_pre)
    active = active_f.astype(BF)
    resid_two = normed_one + plain_dot(active, w_outer) + b_outer
    normed_two, second_pull = jax.vjp(layer_norm, resid_two, g_second, s_second)
    layer_out = normed_two.astype(BF)

    def scattered(value):
        return lax.psum_scatter(value, "ctx", scatter_dimension=0, tiled=True).astype(F32)

    grad_two, grad_second_gain, grad_second_shift = second_pull(out_grad.astype(F32))
    grad_two_low = grad_two.astype(BF)
    grad_outer_bias = jnp.sum(grad_two_low.astype(F32), axis=0)
    grad_outer_weight = rows_dot(active, grad_two_low).astype(BF)
    grad_inner = gelu_pull(cols_dot(grad_two_low, w_outer))[0].astype(BF)
    grad_inner_bias = jnp.sum(grad_inner.astype(F32), axis=0)
    grad_inner_weight = rows_dot(normed_low, grad_inner).astype(BF)
    grad_one = grad_two + cols_dot(grad_inner, w_inner)
    grad_resid_one, grad_first_gain, grad_first_shift = first_pull(grad_one)
    grad_one_low = grad_resid_one.astype(BF)
    grad_output_bias = jnp.sum(grad_one_low.astype(F32), axis=0)
    grad_output_weight = rows_dot(context_rows, grad_one_low).astype(BF)
    slabs = lambda value: value.reshape(devices, -1, m)
    hidden_blocks = grad_inner_weight.shape[1] // m
    late_grads = scattered(
        jnp.concatenate(
            [slabs(grad_outer_weight), slabs(grad_output_weight)]
            + [slabs(grad_inner_weight[:, i * m : (i + 1) * m]) for i in range(hidden_blocks)],
            axis=1,
        )
    )[0]
    outer_rows = outer_weight.shape[0]
    grad_outer_weight = late_grads[:outer_rows]
    late_grads = late_grads[outer_rows:].reshape(1 + hidden_blocks, weight_rows, m)
    grad_output_weight = late_grads[0]
    grad_inner_weight = jnp.concatenate([late_grads[1 + i] for i in range(hidden_blocks)], axis=1)
    context_gradient = cols_dot(grad_one_low, w_output).astype(BF)

    query_low, kv_low, attn_sums = attend_back(near, picks, spans, query_rows, kv_buf, context_gradient)
    grad_x_buf = cols_dot(kv_low, w_kv).astype(BF)
    grad_vectors = jnp.concatenate(
        [
            attn_sums,
            jnp.stack(
                [
                    grad_output_bias, grad_first_gain, grad_first_shift, grad_outer_bias, grad_second_gain,
                    grad_second_shift,
                ]
            ),
            grad_inner_bias.reshape(-1, m),
        ],
        axis=0,
    )
    grad_query_weight, grad_key_weight, grad_value_weight, sums, halo_part = reduce_grads(
        rows_dot(layer_input, query_low).astype(BF).reshape(devices, -1, m),
        rows_dot(x_buf, kv_low).astype(BF).reshape(devices, -1, 2 * m),
        grad_vectors,
        grad_x_buf,
        row_count,
        devices,
    )
    grad_input = grad_resid_one + cols_dot(query_low, w_query) + halo_part
    me = lax.axis_index("ctx")
    own_sums = lax.dynamic_slice_in_dim(sums[:8], me * unit, unit, 1)
    v_query, v_value, v_output, v_gain1, v_shift1, v_outer, v_gain2, v_shift2 = [own_sums[i] for i in range(8)]
    inner_unit = inner_bias.shape[0]
    inner_at = me * inner_unit
    v_inner = lax.dynamic_slice(sums, (8 + inner_at // m, inner_at % m), (1, inner_unit))[0]
    return (
        layer_out, grad_input, grad_query_weight, v_query, grad_key_weight, grad_value_weight, v_value,
        grad_output_weight, v_output, v_gain1, v_shift1, grad_inner_weight, v_inner, grad_outer_weight, v_outer,
        v_gain2, v_shift2,
    )


def solution(mesh):
    rows, line = P("ctx", None), P("ctx")
    in_specs = (
        rows, rows, P(), P("ctx", None, None), rows, line, rows, rows, line, rows, line, line, line, rows, line, rows,
        line, line, line,
    )
    out_specs = (
        rows, rows, rows, line, rows, rows, line, rows, line, line, line, rows, line, rows, line, line, line,
    )
    return jax.shard_map(on_device, mesh=mesh, in_specs=in_specs, out_specs=out_specs, check_vma=False)
```

```python
import functools
import math

import jax
import jax.numpy as jnp
from jax import lax
from jax.experimental import pallas as pl
from jax.experimental.pallas import tpu as pltpu
from jax.sharding import PartitionSpec as P

BLOCK = 64
DOC_MAX = 32
REACH = DOC_MAX - 1
SLOTS = 8
WIDE = SLOTS * BLOCK
CHUNKS = DOC_MAX // SLOTS
LANES = 128

norm_eps = 1e-06
masked_score = -1e30
BF = jnp.bfloat16
F32 = jnp.float32


def layer_norm(hidden, scale_gain, shift_vec):
    row_mean = jnp.mean(hidden, axis=-1, keepdims=True)
    centred = hidden - row_mean
    variance = jnp.mean(centred * centred, axis=-1, keepdims=True)
    return centred * lax.rsqrt(variance + norm_eps) * scale_gain + shift_vec


def gelu_and_slope(inner_pre):
    below = 0.5 + 0.5 * lax.erf(inner_pre * math.sqrt(0.5))
    density = jnp.exp(-0.5 * inner_pre * inner_pre) * (1.0 / math.sqrt(2.0 * math.pi))
    return (inner_pre * below, below + inner_pre * density)


def plain_dot(left, right):
    return jnp.dot(left, right, preferred_element_type=F32)


def rows_dot(left, right):
    return lax.dot_general(left, right, (((0,), (0,)), ((), ())), preferred_element_type=F32)


def cols_dot(left, right):
    return lax.dot_general(left, right, (((1,), (1,)), ((), ())), preferred_element_type=F32)


def doc_layout(doc_starts, block_ids):
    start_blocks = doc_starts // BLOCK
    before = start_blocks[None, :] <= block_ids[:, None]
    doc_ids = jnp.sum(before.astype(jnp.int32), axis=1) - 1
    first_block = jnp.max(jnp.where(before, start_blocks[None, :], -1), axis=1)
    return (doc_ids, first_block)


def link_orders(count):
    bits = count.bit_length() - 1
    assert count == 1 << bits and bits >= 4, count
    high = list(range(bits - 1, 2, -1))
    return [[1] + high + [2, 0], [1, 2] + high + [0], [1] + high[:-1] + [2] + high[-1:] + [0]]


def bit_of(index, bit):
    return (index // (1 << bit)) % 2


def across(index, bit):
    return index + (1 << bit) * (1 - 2 * bit_of(index, bit))


def place_of(index, order):
    return sum(bit_of(index, bit) * (1 << k) for k, bit in enumerate(order))


def remote(source, target, send_sem, recv_sem, device):
    return pltpu.make_async_remote_copy(
        src_ref=source, dst_ref=target, send_sem=send_sem, recv_sem=recv_sem, device_id=(device,),
        device_id_type=pl.DeviceIdType.MESH,
    )


def halo_sizes(own_rows):
    far = REACH * BLOCK - 2 * own_rows
    assert 0 < far <= own_rows, own_rows
    return far, [0] + [far + own_rows * i for i in range(6)]


def halo_links(me, count):
    odd = me % 2
    partner = me - 3 + 6 * odd
    return odd, me >= 2, me < count - 2, (partner >= 0) & (partner < count), partner


def greet(me, bits, count):
    barrier = pltpu.get_barrier_semaphore()

    def hello(device):
        pl.semaphore_signal(barrier, inc=1, device_id=(device,), device_id_type=pl.DeviceIdType.MESH)

    _, has_before, has_after, has_far, partner = halo_links(me, count)
    for bit in range(bits):
        hello(across(me, bit))

    @pl.when(has_before)
    def _():
        hello(me - 2)

    @pl.when(has_after)
    def _():
        hello(me + 2)

    @pl.when(has_far)
    def _():
        hello(partner)

    expected = bits + has_before.astype(jnp.int32) + has_after.astype(jnp.int32) + has_far.astype(jnp.int32)
    pl.semaphore_wait(barrier, expected)


def gather_kernel(
    count, wq_ref, wk_ref, wv_ref, v_ref, x_ref, w_out, v_out, x_out, low_w, low_v, buf_a, buf_b, buf_c, buf_v, zeros, local_sem, out_sem, send_sem,
    recv_sem, halo_send, halo_recv, fill_sem,
):
    me = lax.axis_index("ctx")
    orders = link_orders(count)
    bits = len(orders[0])
    width = wq_ref.shape[1]
    low_w[:, :width] = wq_ref[...].astype(BF)
    for i in range(width // LANES):
        start = width + 2 * i * LANES
        low_w[:, start : start + LANES] = wk_ref[:, i * LANES : (i + 1) * LANES].astype(BF)
        low_w[:, start + LANES : start + 2 * LANES] = wv_ref[:, i * LANES : (i + 1) * LANES].astype(BF)
    low_v[...] = v_ref[...].astype(BF)
    orders = orders + [orders[0]]
    bufs = [buf_a, buf_b, buf_c, buf_v]
    sources = [low_w.at[:, pl.ds(i * width, width)] for i in range(3)] + [low_v]
    places = [place_of(me, order) for order in orders]
    full = x_ref.shape[0]
    part, piece = halo_sizes(full)
    odd, has_before, has_after, has_far, partner = halo_links(me, count)
    sibling = across(me, 0)

    def rows(start, size):
        return x_out.at[pl.ds(pl.multiple_of(start, BLOCK), size), :]

    def halo(index, source, target, device):
        return remote(source, target, halo_send.at[index], halo_recv.at[index], device)

    zeros[...] = jnp.zeros_like(zeros)
    keep_own = pltpu.make_async_copy(x_ref, rows(piece[3], full), local_sem.at[4])
    keep_own.start()
    greet(me, bits, count)
    for i in range(4):
        pltpu.make_async_copy(sources[i], bufs[i].at[places[i]], local_sem.at[i]).start()

    after = halo(0, x_ref, rows(piece[1], full), me + 2)
    before = halo(1, x_ref, rows(piece[5], full), me - 2)
    far_rows = x_ref.at[pl.ds(pl.multiple_of(odd * (full - part), BLOCK), part), :]
    far = halo(2, far_rows, rows((1 - odd) * piece[6], part), partner)
    own = halo(3, x_ref, rows(piece[2] + odd * (piece[4] - piece[2]), full), sibling)
    wide = halo(
        4, rows(piece[5] + odd * (piece[1] - piece[5]), full), rows(piece[4] + odd * (piece[2] - piece[4]), full), sibling
    )
    edge_from = (piece[1] + full - part) * (1 - odd) + piece[5] * odd
    edge = halo(5, rows(edge_from, part), rows(piece[6] * odd, part), sibling)
    has_wide = jnp.where(odd == 1, has_before, has_after)
    has_edge = jnp.where(odd == 1, has_after, has_before)

    for i in range(4):
        pltpu.make_async_copy(sources[i], bufs[i].at[places[i]], local_sem.at[i]).wait()
    copies = [own]
    for k in range(bits):
        stage = []
        for i in range(4):
            held = bufs[i].at[pl.ds((places[i] // (1 << k)) * (1 << k), 1 << k)]
            copy = remote(held, held, send_sem.at[i, k], recv_sem.at[i, k], across(me, orders[i][k]))
            copy.start()
            stage.append(copy)
        for copy in stage:
            copy.wait_recv()
        copies += stage
        if k == 0:
            own.start()
            pl.when(has_after)(after.start)
            pl.when(has_before)(before.start)
            pl.when(has_far)(far.start)

    def put(j, carry):
        for i in range(3):
            pltpu.make_async_copy(
                bufs[i].at[place_of(j, orders[i])], w_out.at[j, :, pl.ds(i * width, width)], out_sem.at[i]
            ).start()
        pltpu.make_async_copy(buf_v.at[place_of(j, orders[3])], v_out.at[j], out_sem.at[3]).start()
        return carry

    lax.fori_loop(0, count, put, 0)

    @pl.when(has_before)
    def _():
        halo(0, x_ref, rows(piece[1], full), sibling).wait_recv()

    @pl.when(has_after)
    def _():
        halo(1, x_ref, rows(piece[5], full), sibling).wait_recv()

    @pl.when(has_wide)
    def _():
        wide.start()

    @pl.when(has_edge)
    def _():
        edge.start()

    def fill(missing, start, size):
        @pl.when(missing)
        def _():
            copy = pltpu.make_async_copy(zeros.at[pl.ds(0, size), :], rows(start, size), fill_sem.at[0])
            copy.start()
            copy.wait()

    fill(jnp.logical_not(has_before), piece[1], full)
    fill(jnp.logical_not(has_after), piece[5], full)
    gets_wide = jnp.where(odd == 1, has_after, has_before)
    gets_edge = jnp.where(odd == 1, has_before, has_after)
    wide_at = piece[2] + odd * (piece[4] - piece[2])
    edge_at = piece[6] * (1 - odd)
    far_at = piece[6] * odd
    own_at = piece[4] + odd * (piece[2] - piece[4])
    fill(jnp.logical_not(gets_wide), wide_at, full)
    fill(jnp.logical_not(gets_edge), edge_at, part)
    fill(jnp.logical_not(has_far), far_at, part)
    halo(3, x_ref, rows(own_at, full), sibling).wait_recv()

    @pl.when(has_far)
    def _():
        halo(2, far_rows, rows(far_at, part), sibling).wait_recv()

    @pl.when(gets_wide)
    def _():
        halo(4, x_ref, rows(wide_at, full), sibling).wait_recv()

    @pl.when(gets_edge)
    def _():
        halo(5, far_rows, rows(edge_at, part), sibling).wait_recv()

    for copy in copies:
        copy.wait_send()
    for exists, copy in ((has_after, after), (has_before, before), (has_far, far), (has_wide, wide), (has_edge, edge)):
        pl.when(exists)(copy.wait_send)
    keep_own.wait()
    for i in range(3):
        pltpu.make_async_copy(bufs[i], w_out.at[:, :, pl.ds(i * width, width)], out_sem.at[i]).wait()
    pltpu.make_async_copy(buf_v, v_out, out_sem.at[3]).wait()


def gather_weights(query, key, value, vectors, own, count):
    rows, columns = query.shape[0], 3 * query.shape[1]
    bits = count.bit_length() - 1
    vmem, any_space = pl.BlockSpec(memory_space=pltpu.VMEM), pl.BlockSpec(memory_space=pl.ANY)
    return pl.pallas_call(
        functools.partial(gather_kernel, count),
        out_shape=(
            jax.ShapeDtypeStruct((count, rows, columns), BF),
            jax.ShapeDtypeStruct((count,) + vectors.shape, BF),
            jax.ShapeDtypeStruct((own.shape[0] + 2 * REACH * BLOCK, own.shape[1]), BF),
        ),
        in_specs=[vmem] * 5,
        out_specs=[any_space, any_space, any_space],
        scratch_shapes=[pltpu.VMEM((rows, columns), BF), pltpu.VMEM(vectors.shape, BF)]
        + [pltpu.VMEM((count, rows, columns // 3), BF)] * 3
        + [
            pltpu.VMEM((count,) + vectors.shape, BF),
            pltpu.VMEM(own.shape, BF),
            pltpu.SemaphoreType.DMA((5,)),
            pltpu.SemaphoreType.DMA((4,)),
            pltpu.SemaphoreType.DMA((4, bits)),
            pltpu.SemaphoreType.DMA((4, bits)),
            pltpu.SemaphoreType.DMA((6,)),
            pltpu.SemaphoreType.DMA((6,)),
            pltpu.SemaphoreType.DMA((1,)),
        ],
        compiler_params=pltpu.CompilerParams(
            collective_id=0, has_side_effects=True, vmem_limit_bytes=60 * 1024 * 1024
        ),
        cost_estimate=pl.CostEstimate(flops=0, bytes_accessed=200_000_000, transcendentals=0),
        name="gather_weights",
    )(query, key, value, vectors, own)


def reduce_kernel(
    count, q_ref, kv_ref, v_ref, x_ref, wq_out, wk_out, wv_out, v_out, x_out, buf_a, buf_b, buf_c, got_a, got_b, got_c, sum_v, got_v,
    left, mid, right, e_own, e_wide, e_edge, e_far, from_after, from_before, load_sem, send_sem, recv_sem, halo_send,
    halo_recv,
):
    me = lax.axis_index("ctx")
    orders = link_orders(count)
    bits = len(orders[0])
    bufs, gots = [buf_a, buf_b, buf_c], [got_a, got_b, got_c]
    width = q_ref.shape[2]
    full = left.shape[0]
    part, piece = halo_sizes(full)
    odd, has_before, has_after, has_far, partner = halo_links(me, count)
    sibling = across(me, 0)

    def rows(start, size):
        return x_ref.at[pl.ds(pl.multiple_of(start, BLOCK), size), :]

    def halo(index, source, target, device):
        return remote(source, target, halo_send.at[index], halo_recv.at[index], device)

    loads = [
        pltpu.make_async_copy(rows(piece[1], full), left, load_sem.at[4]),
        pltpu.make_async_copy(rows(piece[3], full), mid, load_sem.at[5]),
        pltpu.make_async_copy(rows(piece[5], full), right, load_sem.at[6]),
    ]
    for copy in loads:
        copy.start()

    def load(j, carry):
        pltpu.make_async_copy(q_ref.at[j], bufs[0].at[place_of(j, orders[0])], load_sem.at[0]).start()
        for i in (1, 2):
            pltpu.make_async_copy(
                kv_ref.at[j, :, pl.ds((i - 1) * width, width)], bufs[i].at[place_of(j, orders[i])], load_sem.at[i]
            ).start()
        return carry

    lax.fori_loop(0, count, load, 0)
    first_sum = pltpu.make_async_copy(v_ref, sum_v.at[0], load_sem.at[3])
    first_sum.start()
    greet(me, bits, count)

    swaps = [
        halo(3, rows(piece[2] + odd * (piece[4] - piece[2]), full), e_wide, sibling),
        halo(4, rows(piece[6] * (1 - odd), part), e_edge, sibling),
        halo(5, rows(piece[4] + odd * (piece[2] - piece[4]), full), e_own, sibling),
    ]
    for copy in swaps:
        copy.start()
    far = halo(2, rows(piece[6] * odd, part), e_far, partner)

    @pl.when(has_far)
    def _():
        far.start()

    for copy in loads:
        copy.wait()
    swaps[0].wait_recv()
    swaps[1].wait_recv()

    def add_into(target, start, source, size):
        def add(j, carry):
            at = pl.ds(pl.multiple_of(start + j * BLOCK, BLOCK), BLOCK)
            total = target[at, :].astype(F32) + source[pl.ds(pl.multiple_of(j * BLOCK, BLOCK), BLOCK), :].astype(F32)
            target[at, :] = total.astype(target.dtype)
            return carry

        lax.fori_loop(0, size // BLOCK, add, 0)

    @pl.when(odd == 0)
    def _():
        add_into(left, full - part, e_edge, part)
        add_into(right, 0, e_wide, full)

    @pl.when(odd == 1)
    def _():
        add_into(left, 0, e_wide, full)
        add_into(right, 0, e_edge, part)

    before = halo(0, left, from_after, me - 2)
    after = halo(1, right, from_before, me + 2)

    @pl.when(has_before)
    def _():
        before.start()

    @pl.when(has_after)
    def _():
        after.start()

    for i in range(3):
        source = q_ref if i == 0 else kv_ref.at[:, :, pl.ds((i - 1) * width, width)]
        pltpu.make_async_copy(source, bufs[i], load_sem.at[i]).wait()
    first_sum.wait()
    places = [place_of(me, order) for order in orders]
    copies = []
    for k in range(bits):
        bit = bits - 1 - k
        half = 1 << bit
        offset = count - 2 * half
        stage = []
        for i in range(3):
            keep = (places[i] // half) * half
            give = keep + half * (1 - 2 * bit_of(places[i], bit))
            copy = remote(
                bufs[i].at[pl.ds(give, half)], gots[i].at[pl.ds(offset, half)], send_sem.at[i, k], recv_sem.at[i, k],
                across(me, orders[i][bit]),
            )
            copy.start()
            stage.append(copy)
        copy = remote(sum_v.at[k], got_v.at[k], send_sem.at[3, k], recv_sem.at[3, k], across(me, orders[0][bit]))
        copy.start()
        stage.append(copy)
        for i in range(3):
            stage[i].wait_recv()
            keep = (places[i] // half) * half
            if k == bits - 1:
                total = bufs[i][keep].astype(F32) + gots[i][offset].astype(F32)
                if i == 0:
                    wq_out[...] = total
                else:
                    for j in range(width // LANES):
                        place = ((i - 1) * width // LANES + j) // 2 * LANES
                        target = wv_out if ((i - 1) * width // LANES + j) % 2 else wk_out
                        target[:, place : place + LANES] = total[:, j * LANES : (j + 1) * LANES]
            else:

                def add(j, carry, i=i, keep=keep, offset=offset):
                    total = bufs[i][keep + j].astype(F32) + gots[i][offset + j].astype(F32)
                    bufs[i][keep + j] = total.astype(BF)
                    return carry

                lax.fori_loop(0, half, add, 0)
        stage[3].wait_recv()
        if k == bits - 1:
            v_out[...] = sum_v[k] + got_v[k]
        else:
            sum_v[k + 1] = sum_v[k] + got_v[k]
        copies += stage

    swaps[2].wait_recv()

    def start_sum(j, carry):
        at = pl.ds(pl.multiple_of(j * BLOCK, BLOCK), BLOCK)
        x_out[at, :] = mid[at, :].astype(F32) + e_own[at, :].astype(F32)
        return carry

    lax.fori_loop(0, full // BLOCK, start_sum, 0)

    @pl.when(has_far)
    def _():
        far.wait_recv()
        add_into(x_out, odd * (full - part), e_far, part)

    @pl.when(has_after)
    def _():
        before.wait_recv()
        add_into(x_out, 0, from_after, full)

    @pl.when(has_before)
    def _():
        after.wait_recv()
        add_into(x_out, 0, from_before, full)

    for copy in copies + swaps:
        copy.wait_send()
    for exists, copy in ((has_after, after), (has_before, before), (has_far, far)):
        pl.when(exists)(copy.wait_send)


def reduce_grads(query_grads, kv_grads, vectors, halo_grads, own_rows, count):
    _, rows, columns = query_grads.shape
    bits = count.bit_length() - 1
    vmem, any_space = pl.BlockSpec(memory_space=pltpu.VMEM), pl.BlockSpec(memory_space=pl.ANY)
    slabs = pltpu.VMEM((count, rows, columns), BF)
    stages = pltpu.VMEM((bits,) + vectors.shape, F32)
    part, _ = halo_sizes(own_rows)
    whole, piece = pltpu.VMEM((own_rows, columns), BF), pltpu.VMEM((part, columns), BF)
    return pl.pallas_call(
        functools.partial(reduce_kernel, count),
        out_shape=(
            jax.ShapeDtypeStruct((rows, columns), F32),
            jax.ShapeDtypeStruct((rows, columns), F32),
            jax.ShapeDtypeStruct((rows, columns), F32),
            jax.ShapeDtypeStruct(vectors.shape, F32),
            jax.ShapeDtypeStruct((own_rows, columns), F32),
        ),
        in_specs=[any_space, any_space, vmem, any_space],
        out_specs=[vmem] * 5,
        scratch_shapes=[slabs] * 6
        + [stages, stages, whole, whole, whole, whole, whole, piece, piece, whole, whole]
        + [
            pltpu.SemaphoreType.DMA((7,)),
            pltpu.SemaphoreType.DMA((4, bits)),
            pltpu.SemaphoreType.DMA((4, bits)),
            pltpu.SemaphoreType.DMA((6,)),
            pltpu.SemaphoreType.DMA((6,)),
        ],
        compiler_params=pltpu.CompilerParams(
            collective_id=1, has_side_effects=True, vmem_limit_bytes=60 * 1024 * 1024
        ),
        cost_estimate=pl.CostEstimate(flops=0, bytes_accessed=200_000_000, transcendentals=0),
        name="reduce_grads",
    )(query_grads, kv_grads, vectors, halo_grads)


def low_half():
    return lax.broadcasted_iota(jnp.int32, (BLOCK, LANES), 1) < LANES // 2


def split_pair(rows):
    half = low_half()
    zero = jnp.zeros_like(rows)
    return jnp.concatenate([jnp.where(half, rows, zero), jnp.where(half, zero, rows)], axis=0)


def join_pair(rows):
    return jnp.where(low_half(), rows[:BLOCK], rows[BLOCK:])


KEY, VALUE = slice(0, LANES), slice(LANES, 2 * LANES)


def block_at(ref, position, side):
    return ref[pl.ds(pl.multiple_of(position * BLOCK, BLOCK), BLOCK), side]


def slots_of(near_ref, rand_ref, block, pair, heads):
    shared = [near_ref[block * 8 + i] for i in range(5)]
    at = (block * heads + 2 * pair) * 3
    chosen = [(rand_ref[at + i], rand_ref[at + 3 + i]) for i in range(3)]
    return shared, chosen


def slot_rows(ref, side, shared, chosen):
    half = low_half()
    parts = [block_at(ref, i, side) for i in shared]
    parts += [jnp.where(half, block_at(ref, a, side), block_at(ref, b, side)) for a, b in chosen]
    return jnp.concatenate(parts, axis=0)


def slot_bias(near_ref, block):
    after = jnp.where(near_ref[block * 8 + 5] > 0, 0.0, masked_score).astype(F32)
    lead = jnp.where(near_ref[block * 8 + 6] > 0, 0.0, masked_score).astype(F32)
    return after, lead


def masked(scores, near_ref, block):
    after, lead = slot_bias(near_ref, block)
    return jnp.concatenate(
        [
            scores[: 2 * BLOCK],
            scores[2 * BLOCK : 3 * BLOCK] + after,
            scores[3 * BLOCK : 4 * BLOCK],
            scores[4 * BLOCK : 5 * BLOCK] + lead,
            scores[5 * BLOCK :],
        ],
        axis=0,
    )


def forward_kernel(heads, own_blocks, near_ref, rand_ref, glob_ref, q_ref, kv_ref, o_ref, s_ref):
    pair = pl.program_id(0)

    def regular(block, carry):
        rows = pl.ds(pl.multiple_of(block * BLOCK, BLOCK), BLOCK)
        shared, chosen = slots_of(near_ref, rand_ref, block, pair, heads)
        queries = split_pair(q_ref[rows, :] * 0.125)
        scores = masked(cols_dot(slot_rows(kv_ref, KEY, shared, chosen), queries), near_ref, block)
        weights = jnp.exp(scores - jnp.max(scores, axis=0, keepdims=True))
        probs = weights * (1.0 / jnp.sum(weights, axis=0, keepdims=True))
        mixed = rows_dot(probs.astype(BF), slot_rows(kv_ref, VALUE, shared, chosen))
        o_ref[rows, :] = join_pair(mixed).astype(BF)
        return carry

    lax.fori_loop(0, own_blocks, regular, 0, unroll=own_blocks)

    def whole(block, carry):
        @pl.when(glob_ref[block * 4] > 0)
        def _():
            rows = pl.ds(pl.multiple_of(block * BLOCK, BLOCK), BLOCK)
            first = glob_ref[block * 4 + 1]
            length = glob_ref[block * 4 + 2]
            queries = split_pair(q_ref[rows, :] * 0.125)
            slot_id = lax.broadcasted_iota(jnp.int32, (WIDE, LANES), 0) // BLOCK

            def score(step, top):
                at = pl.ds(pl.multiple_of((first + step * SLOTS) * BLOCK, BLOCK), WIDE)
                scores = cols_dot(kv_ref[at, KEY], queries)
                scores = jnp.where(slot_id < length - step * SLOTS, scores, masked_score)
                s_ref[step] = scores
                return jnp.maximum(top, jnp.max(scores, axis=0, keepdims=True))

            top = lax.fori_loop(0, CHUNKS, score, jnp.full((1, LANES), masked_score, F32), unroll=True)

            def mix(step, kept):
                total, acc = kept
                at = pl.ds(pl.multiple_of((first + step * SLOTS) * BLOCK, BLOCK), WIDE)
                weights = jnp.exp(s_ref[step] - top)
                return (
                    total + jnp.sum(weights, axis=0, keepdims=True),
                    acc + rows_dot(weights.astype(BF), kv_ref[at, VALUE]),
                )

            total, acc = lax.fori_loop(0, CHUNKS, mix, (jnp.zeros((1, LANES), F32), jnp.zeros((LANES, LANES), F32)), unroll=True)
            scale = jnp.transpose(jnp.broadcast_to(1.0 / total, (LANES, LANES)))
            o_ref[rows, :] = join_pair(acc * scale).astype(BF)

        return carry

    lax.fori_loop(0, own_blocks, whole, 0)


def backward_kernel(
    heads, own_blocks, near_ref, rand_ref, glob_ref, q_ref, kv_ref, c_ref,
    dq_ref, dkv_ref, sum_ref, dk_acc, dv_acc, s_ref, p_ref,
):
    pair = pl.program_id(0)
    dk_acc[...] = jnp.zeros_like(dk_acc)
    dv_acc[...] = jnp.zeros_like(dv_acc)
    half = low_half()

    def add_rows(acc, shared, chosen, update):
        for i, position in enumerate(shared):
            at = pl.ds(pl.multiple_of(position * BLOCK, BLOCK), BLOCK)
            acc[at, :] += update[i * BLOCK : (i + 1) * BLOCK]
        for i, (one, two) in enumerate(chosen):
            piece = update[(5 + i) * BLOCK : (6 + i) * BLOCK]
            at = pl.ds(pl.multiple_of(one * BLOCK, BLOCK), BLOCK)
            acc[at, :] += jnp.where(half, piece, 0.0)
            at = pl.ds(pl.multiple_of(two * BLOCK, BLOCK), BLOCK)
            acc[at, :] += jnp.where(half, 0.0, piece)

    def regular(block, carry):
        rows = pl.ds(pl.multiple_of(block * BLOCK, BLOCK), BLOCK)
        shared, chosen = slots_of(near_ref, rand_ref, block, pair, heads)
        queries = split_pair(q_ref[rows, :] * 0.125)
        slope = c_ref[rows, :]
        slope = split_pair(jnp.where(glob_ref[block * 4] > 0, jnp.zeros_like(slope), slope))
        keys = slot_rows(kv_ref, KEY, shared, chosen)
        scores = masked(cols_dot(keys, queries), near_ref, block)
        weights = jnp.exp(scores - jnp.max(scores, axis=0, keepdims=True))
        probs = weights * (1.0 / jnp.sum(weights, axis=0, keepdims=True))
        dprobs = cols_dot(slot_rows(kv_ref, VALUE, shared, chosen), slope)
        inner = jnp.sum(probs * dprobs, axis=0, keepdims=True)
        dscores = (probs * (dprobs - inner)).astype(BF)
        dq_ref[rows, :] = (join_pair(rows_dot(dscores, keys)) * 0.125).astype(BF)
        add_rows(dk_acc, shared, chosen, plain_dot(dscores, queries))
        add_rows(dv_acc, shared, chosen, plain_dot(probs.astype(BF), slope))
        return carry

    lax.fori_loop(0, own_blocks, regular, 0, unroll=6)

    def whole(block, carry):
        @pl.when(glob_ref[block * 4] > 0)
        def _():
            rows = pl.ds(pl.multiple_of(block * BLOCK, BLOCK), BLOCK)
            first = glob_ref[block * 4 + 1]
            length = glob_ref[block * 4 + 2]
            queries = split_pair(q_ref[rows, :] * 0.125)
            slope = split_pair(c_ref[rows, :])
            slot_id = lax.broadcasted_iota(jnp.int32, (WIDE, LANES), 0) // BLOCK

            def score(step, top):
                at = pl.ds(pl.multiple_of((first + step * SLOTS) * BLOCK, BLOCK), WIDE)
                scores = cols_dot(kv_ref[at, KEY], queries)
                scores = jnp.where(slot_id < length - step * SLOTS, scores, masked_score)
                s_ref[step] = scores
                p_ref[step] = cols_dot(kv_ref[at, VALUE], slope)
                return jnp.maximum(top, jnp.max(scores, axis=0, keepdims=True))

            top = lax.fori_loop(0, CHUNKS, score, jnp.full((1, LANES), masked_score, F32), unroll=True)

            def weigh(step, kept):
                total, inner = kept
                weights = jnp.exp(s_ref[step] - top)
                s_ref[step] = weights
                return (
                    total + jnp.sum(weights, axis=0, keepdims=True),
                    inner + jnp.sum(weights * p_ref[step], axis=0, keepdims=True),
                )

            zero_row = jnp.zeros((1, LANES), F32)
            total, inner = lax.fori_loop(0, CHUNKS, weigh, (zero_row, zero_row), unroll=True)
            scale = 1.0 / total
            inner = inner * scale

            def spread(step, dq_sum):
                at = pl.ds(pl.multiple_of((first + step * SLOTS) * BLOCK, BLOCK), WIDE)
                probs = s_ref[step] * scale
                dscores = (probs * (p_ref[step] - inner)).astype(BF)
                dk_acc[at, :] += plain_dot(dscores, queries)
                dv_acc[at, :] += plain_dot(probs.astype(BF), slope)
                return dq_sum + rows_dot(dscores, kv_ref[at, KEY])

            dq_sum = lax.fori_loop(0, CHUNKS, spread, jnp.zeros((LANES, LANES), F32), unroll=True)
            dq_ref[rows, :] = (join_pair(dq_sum) * 0.125).astype(BF)

        return carry

    lax.fori_loop(0, own_blocks, whole, 0)
    dkv_ref[:, KEY] = dk_acc[...].astype(BF)
    dv_low = dv_acc[...].astype(BF)
    dkv_ref[:, VALUE] = dv_low
    sum_ref[0:1, :] = jnp.sum(dq_ref[...].astype(F32), axis=0, keepdims=True)
    sum_ref[1:2, :] = jnp.sum(dv_low.astype(F32), axis=0, keepdims=True)


def attention_calls(row_count, model_width, heads, buf_rows):
    own_blocks = row_count // BLOCK
    pairs = heads // 2
    own = lambda: pl.BlockSpec((row_count, LANES), lambda p, *_: (0, p))
    both = lambda: pl.BlockSpec((buf_rows, 2 * LANES), lambda p, *_: (0, p))
    params = lambda: pltpu.CompilerParams(vmem_limit_bytes=48 * 1024 * 1024)
    forward = pl.pallas_call(
        functools.partial(forward_kernel, heads, own_blocks),
        out_shape=jax.ShapeDtypeStruct((row_count, model_width), BF),
        grid_spec=pltpu.PrefetchScalarGridSpec(
            num_scalar_prefetch=3,
            grid=(pairs,),
            in_specs=[own(), both()],
            out_specs=own(),
            scratch_shapes=[pltpu.VMEM((CHUNKS, WIDE, LANES), F32)],
        ),
        compiler_params=params(),
        cost_estimate=pl.CostEstimate(
            flops=4 * row_count * WIDE * 2 * model_width, bytes_accessed=4 * buf_rows * model_width,
            transcendentals=row_count * WIDE * heads,
        ),
        name="attend_forward",
    )
    backward = pl.pallas_call(
        functools.partial(backward_kernel, heads, own_blocks),
        out_shape=(
            jax.ShapeDtypeStruct((row_count, model_width), BF),
            jax.ShapeDtypeStruct((buf_rows, 2 * model_width), BF),
            jax.ShapeDtypeStruct((2, model_width), F32),
        ),
        grid_spec=pltpu.PrefetchScalarGridSpec(
            num_scalar_prefetch=3,
            grid=(pairs,),
            in_specs=[own(), both(), own()],
            out_specs=[own(), both(), pl.BlockSpec((2, LANES), lambda p, *_: (0, p))],
            scratch_shapes=[
                pltpu.VMEM((buf_rows, LANES), F32),
                pltpu.VMEM((buf_rows, LANES), F32),
                pltpu.VMEM((CHUNKS, WIDE, LANES), F32),
                pltpu.VMEM((CHUNKS, WIDE, LANES), F32),
            ],
        ),
        compiler_params=params(),
        cost_estimate=pl.CostEstimate(
            flops=10 * row_count * WIDE * 2 * model_width, bytes_accessed=8 * buf_rows * model_width,
            transcendentals=row_count * WIDE * heads,
        ),
        name="attend_backward",
    )
    return forward, backward


def interleaved(one, two):
    return jnp.concatenate(
        [side[..., i : i + LANES] for i in range(0, one.shape[-1], LANES) for side in (one, two)], axis=-1
    )


def on_device(
    layer_input, out_grad, doc_starts, rand_blocks, query_weight, query_bias, key_weight, value_weight,
    value_bias, output_weight, output_bias, first_gain, first_shift, inner_weight, inner_bias,
    outer_weight, outer_bias, second_gain, second_shift,
):
    row_count, model_width = layer_input.shape
    head_count = rand_blocks.shape[1]
    devices = lax.axis_size("ctx")
    own_blocks = row_count // BLOCK
    buf_blocks = 2 * REACH + own_blocks
    own_first = lax.axis_index("ctx") * own_blocks
    buf_first = own_first - REACH
    block_total = own_blocks * devices
    own_ids = own_first + jnp.arange(own_blocks, dtype=jnp.int32)
    own_doc, own_start = doc_layout(doc_starts, own_ids)
    next_doc = doc_layout(doc_starts, own_ids + 1)[0]
    start_blocks = doc_starts // BLOCK
    later = start_blocks[None, :] > own_ids[:, None]
    doc_end = jnp.min(jnp.where(later, start_blocks[None, :], block_total), axis=1)
    glob_own = own_ids - own_start < 2

    def local(ids):
        return jnp.clip(ids - buf_first, 0, buf_blocks - 1).astype(jnp.int32)

    near = jnp.stack(
        [
            local(own_ids - 1),
            local(own_ids),
            local(own_ids + 1),
            local(own_start),
            local(own_start + 1),
            ((own_ids + 1 < block_total) & (next_doc == own_doc)).astype(jnp.int32),
            (own_ids - own_start > 2).astype(jnp.int32),
            jnp.zeros_like(own_ids),
        ],
        axis=1,
    ).reshape(-1)
    picks = local(rand_blocks).reshape(-1)
    spans = jnp.stack(
        [glob_own.astype(jnp.int32), local(own_start), doc_end - own_start, jnp.zeros_like(own_ids)], axis=1
    ).reshape(-1)
    attend, attend_back = attention_calls(row_count, model_width, head_count, buf_blocks * BLOCK)
    m = model_width
    unit = query_bias.shape[0]
    weight_rows = query_weight.shape[0]

    def gathered(value):
        return lax.all_gather(value, "ctx", axis=0, tiled=True)

    vectors = jnp.concatenate(
        [
            query_bias, value_bias, output_bias, first_gain, first_shift, outer_bias, second_gain, second_shift,
            inner_bias,
        ]
    )
    lane_pad = -vectors.shape[0] % LANES
    first_all, vector_all, x_buf = gather_weights(
        query_weight, key_weight, value_weight, jnp.pad(vectors, (0, lane_pad))[None, :], layer_input, devices
    )
    w_qkv = first_all.reshape(m, 3 * m)
    vector_all = vector_all[:, 0].astype(F32)
    b_query, b_value, b_output, g_first, s_first, b_outer, g_second, s_second = [
        vector_all[:, i * unit : (i + 1) * unit].reshape(-1) for i in range(8)
    ]
    b_inner = vector_all[:, 8 * unit : 8 * unit + inner_bias.shape[0]].reshape(-1)
    w_late = gathered(jnp.concatenate([output_weight, inner_weight], axis=1).astype(BF))
    w_output, w_inner = w_late[:, :m], w_late[:, m:]
    w_outer = gathered(outer_weight.astype(BF))
    w_query, w_kv = w_qkv[:, :m], w_qkv[:, m:]

    query_rows = (plain_dot(layer_input, w_query) + b_query).astype(BF)
    kv_buf = (plain_dot(x_buf, w_kv) + interleaved(jnp.zeros_like(b_value), b_value)).astype(BF)
    context_rows = attend(near, picks, spans, query_rows, kv_buf)

    input_float = layer_input.astype(F32)
    resid_one = input_float + plain_dot(context_rows, w_output) + b_output
    normed_one, first_pull = jax.vjp(layer_norm, resid_one, g_first, s_first)
    normed_low = normed_one.astype(BF)
    inner_pre = plain_dot(normed_low, w_inner) + b_inner
    active, active_slope = gelu_and_slope(inner_pre)
    active, active_slope = lax.optimization_barrier((active.astype(BF), active_slope))
    resid_two = normed_one + plain_dot(active, w_outer) + b_outer
    normed_two, second_pull = jax.vjp(layer_norm, resid_two, g_second, s_second)
    layer_out = normed_two.astype(BF)

    def scattered(value):
        return lax.psum_scatter(value, "ctx", scatter_dimension=0, tiled=True).astype(F32)

    grad_two, grad_second_gain, grad_second_shift = second_pull(out_grad.astype(F32))
    grad_two_low = grad_two.astype(BF)
    grad_outer_bias = jnp.sum(grad_two_low.astype(F32), axis=0)
    grad_outer_weight = rows_dot(active, grad_two_low).astype(BF)
    grad_inner = (cols_dot(grad_two_low, w_outer) * active_slope).astype(BF)
    grad_inner_bias = jnp.sum(grad_inner.astype(F32), axis=0)
    grad_inner_weight = rows_dot(normed_low, grad_inner).astype(BF)
    grad_one = grad_two + cols_dot(grad_inner, w_inner)
    grad_resid_one, grad_first_gain, grad_first_shift = first_pull(grad_one)
    grad_one_low = grad_resid_one.astype(BF)
    grad_output_bias = jnp.sum(grad_one_low.astype(F32), axis=0)
    grad_output_weight = rows_dot(context_rows, grad_one_low).astype(BF)
    slabs = lambda value: value.reshape(devices, -1, m)
    hidden_blocks = grad_inner_weight.shape[1] // m
    late_grads = scattered(
        jnp.concatenate(
            [slabs(grad_outer_weight), slabs(grad_output_weight)]
            + [slabs(grad_inner_weight[:, i * m : (i + 1) * m]) for i in range(hidden_blocks)],
            axis=1,
        )
    )[0]
    outer_rows = outer_weight.shape[0]
    grad_outer_weight = late_grads[:outer_rows]
    late_grads = late_grads[outer_rows:].reshape(1 + hidden_blocks, weight_rows, m)
    grad_output_weight = late_grads[0]
    grad_inner_weight = jnp.concatenate([late_grads[1 + i] for i in range(hidden_blocks)], axis=1)
    context_gradient = cols_dot(grad_one_low, w_output).astype(BF)

    query_low, kv_low, attn_sums = attend_back(near, picks, spans, query_rows, kv_buf, context_gradient)
    grad_x_buf = cols_dot(kv_low, w_kv).astype(BF)
    grad_vectors = jnp.concatenate(
        [
            attn_sums,
            jnp.stack(
                [
                    grad_output_bias, grad_first_gain, grad_first_shift, grad_outer_bias, grad_second_gain,
                    grad_second_shift,
                ]
            ),
            grad_inner_bias.reshape(-1, m),
        ],
        axis=0,
    )
    grad_query_weight, grad_key_weight, grad_value_weight, sums, halo_part = reduce_grads(
        rows_dot(layer_input, query_low).astype(BF).reshape(devices, -1, m),
        rows_dot(x_buf, kv_low).astype(BF).reshape(devices, -1, 2 * m),
        grad_vectors,
        grad_x_buf,
        row_count,
        devices,
    )
    grad_input = grad_resid_one + cols_dot(query_low, w_query) + halo_part
    me = lax.axis_index("ctx")
    own_sums = lax.dynamic_slice_in_dim(sums[:8], me * unit, unit, 1)
    v_query, v_value, v_output, v_gain1, v_shift1, v_outer, v_gain2, v_shift2 = [own_sums[i] for i in range(8)]
    inner_unit = inner_bias.shape[0]
    inner_at = me * inner_unit
    v_inner = lax.dynamic_slice(sums, (8 + inner_at // m, inner_at % m), (1, inner_unit))[0]
    return (
        layer_out, grad_input, grad_query_weight, v_query, grad_key_weight, grad_value_weight, v_value,
        grad_output_weight, v_output, v_gain1, v_shift1, grad_inner_weight, v_inner, grad_outer_weight, v_outer,
        v_gain2, v_shift2,
    )


def solution(mesh):
    rows, line = P("ctx", None), P("ctx")
    in_specs = (
        rows, rows, P(), P("ctx", None, None), rows, line, rows, rows, line, rows, line, line, line, rows, line, rows,
        line, line, line,
    )
    out_specs = (
        rows, rows, rows, line, rows, rows, line, rows, line, line, line, rows, line, rows, line, line, line,
    )
    return jax.shard_map(on_device, mesh=mesh, in_specs=in_specs, out_specs=out_specs, check_vma=False)
```

```python
import functools
import math

import jax
import jax.numpy as jnp
from jax import lax
from jax.experimental import pallas as pl
from jax.experimental.pallas import tpu as pltpu
from jax.sharding import PartitionSpec as P

BLOCK = 64
DOC_MAX = 32
REACH = DOC_MAX - 1
SLOTS = 8
WIDE = SLOTS * BLOCK
CHUNKS = DOC_MAX // SLOTS
LANES = 128

norm_eps = 1e-06
masked_score = -1e30
BF = jnp.bfloat16
F32 = jnp.float32


def layer_norm(hidden, scale_gain, shift_vec):
    row_mean = jnp.mean(hidden, axis=-1, keepdims=True)
    centred = hidden - row_mean
    variance = jnp.mean(centred * centred, axis=-1, keepdims=True)
    return centred * lax.rsqrt(variance + norm_eps) * scale_gain + shift_vec


def gelu_and_slope(inner_pre):
    below = 0.5 + 0.5 * lax.erf(inner_pre * math.sqrt(0.5))
    density = jnp.exp(-0.5 * inner_pre * inner_pre) * (1.0 / math.sqrt(2.0 * math.pi))
    return (inner_pre * below, below + inner_pre * density)


def plain_dot(left, right):
    return jnp.dot(left, right, preferred_element_type=F32)


def rows_dot(left, right):
    return lax.dot_general(left, right, (((0,), (0,)), ((), ())), preferred_element_type=F32)


def cols_dot(left, right):
    return lax.dot_general(left, right, (((1,), (1,)), ((), ())), preferred_element_type=F32)


def doc_layout(doc_starts, block_ids):
    start_blocks = doc_starts // BLOCK
    before = start_blocks[None, :] <= block_ids[:, None]
    doc_ids = jnp.sum(before.astype(jnp.int32), axis=1) - 1
    first_block = jnp.max(jnp.where(before, start_blocks[None, :], -1), axis=1)
    return (doc_ids, first_block)


def link_orders(count):
    bits = count.bit_length() - 1
    assert count == 1 << bits and bits >= 4, count
    high = list(range(bits - 1, 2, -1))
    return [[1] + high + [2, 0], [1, 2] + high + [0], [1] + high[:-1] + [2] + high[-1:] + [0]]


def bit_of(index, bit):
    return (index // (1 << bit)) % 2


def across(index, bit):
    return index + (1 << bit) * (1 - 2 * bit_of(index, bit))


def place_of(index, order):
    return sum(bit_of(index, bit) * (1 << k) for k, bit in enumerate(order))


def remote(source, target, send_sem, recv_sem, device):
    return pltpu.make_async_remote_copy(
        src_ref=source, dst_ref=target, send_sem=send_sem, recv_sem=recv_sem, device_id=(device,),
        device_id_type=pl.DeviceIdType.MESH,
    )


def halo_sizes(own_rows):
    far = REACH * BLOCK - 2 * own_rows
    assert 0 < far <= own_rows, own_rows
    return far, [0] + [far + own_rows * i for i in range(6)]


def halo_links(me, count):
    odd = me % 2
    partner = me - 3 + 6 * odd
    return odd, me >= 2, me < count - 2, (partner >= 0) & (partner < count), partner


def greet(me, bits, count):
    barrier = pltpu.get_barrier_semaphore()

    def hello(device):
        pl.semaphore_signal(barrier, inc=1, device_id=(device,), device_id_type=pl.DeviceIdType.MESH)

    _, has_before, has_after, has_far, partner = halo_links(me, count)
    for bit in range(bits):
        hello(across(me, bit))

    @pl.when(has_before)
    def _():
        hello(me - 2)

    @pl.when(has_after)
    def _():
        hello(me + 2)

    @pl.when(has_far)
    def _():
        hello(partner)

    expected = bits + has_before.astype(jnp.int32) + has_after.astype(jnp.int32) + has_far.astype(jnp.int32)
    pl.semaphore_wait(barrier, expected)


def gather_kernel(
    count, wq_ref, wk_ref, wv_ref, v_ref, x_ref, w_out, v_out, x_out, low_w, low_v, buf_a, buf_b, buf_c, buf_v, zeros, local_sem, out_sem, send_sem,
    recv_sem, halo_send, halo_recv, fill_sem,
):
    me = lax.axis_index("ctx")
    orders = link_orders(count)
    bits = len(orders[0])
    width = wq_ref.shape[1]
    low_w[:, :width] = wq_ref[...].astype(BF)
    for i in range(width // LANES):
        start = width + 2 * i * LANES
        low_w[:, start : start + LANES] = wk_ref[:, i * LANES : (i + 1) * LANES].astype(BF)
        low_w[:, start + LANES : start + 2 * LANES] = wv_ref[:, i * LANES : (i + 1) * LANES].astype(BF)
    low_v[...] = v_ref[...].astype(BF)
    orders = orders + [orders[0]]
    bufs = [buf_a, buf_b, buf_c, buf_v]
    sources = [low_w.at[:, pl.ds(i * width, width)] for i in range(3)] + [low_v]
    places = [place_of(me, order) for order in orders]
    full = x_ref.shape[0]
    part, piece = halo_sizes(full)
    odd, has_before, has_after, has_far, partner = halo_links(me, count)
    sibling = across(me, 0)

    def rows(start, size):
        return x_out.at[pl.ds(pl.multiple_of(start, BLOCK), size), :]

    def halo(index, source, target, device):
        return remote(source, target, halo_send.at[index], halo_recv.at[index], device)

    zeros[...] = jnp.zeros_like(zeros)
    keep_own = pltpu.make_async_copy(x_ref, rows(piece[3], full), local_sem.at[4])
    keep_own.start()
    greet(me, bits, count)
    for i in range(4):
        pltpu.make_async_copy(sources[i], bufs[i].at[places[i]], local_sem.at[i]).start()

    after = halo(0, x_ref, rows(piece[1], full), me + 2)
    before = halo(1, x_ref, rows(piece[5], full), me - 2)
    far_rows = x_ref.at[pl.ds(pl.multiple_of(odd * (full - part), BLOCK), part), :]
    far = halo(2, far_rows, rows((1 - odd) * piece[6], part), partner)
    own = halo(3, x_ref, rows(piece[2] + odd * (piece[4] - piece[2]), full), sibling)
    wide = halo(
        4, rows(piece[5] + odd * (piece[1] - piece[5]), full), rows(piece[4] + odd * (piece[2] - piece[4]), full), sibling
    )
    edge_from = (piece[1] + full - part) * (1 - odd) + piece[5] * odd
    edge = halo(5, rows(edge_from, part), rows(piece[6] * odd, part), sibling)
    has_wide = jnp.where(odd == 1, has_before, has_after)
    has_edge = jnp.where(odd == 1, has_after, has_before)

    for i in range(4):
        pltpu.make_async_copy(sources[i], bufs[i].at[places[i]], local_sem.at[i]).wait()
    copies = [own]
    for k in range(bits):
        stage = []
        for i in range(4):
            held = bufs[i].at[pl.ds((places[i] // (1 << k)) * (1 << k), 1 << k)]
            copy = remote(held, held, send_sem.at[i, k], recv_sem.at[i, k], across(me, orders[i][k]))
            copy.start()
            stage.append(copy)
        for copy in stage:
            copy.wait_recv()
        copies += stage
        if k == 0:
            own.start()
            pl.when(has_after)(after.start)
            pl.when(has_before)(before.start)
            pl.when(has_far)(far.start)

    def put(j, carry):
        for i in range(3):
            pltpu.make_async_copy(
                bufs[i].at[place_of(j, orders[i])], w_out.at[j, :, pl.ds(i * width, width)], out_sem.at[i]
            ).start()
        pltpu.make_async_copy(buf_v.at[place_of(j, orders[3])], v_out.at[j], out_sem.at[3]).start()
        return carry

    lax.fori_loop(0, count, put, 0)

    @pl.when(has_before)
    def _():
        halo(0, x_ref, rows(piece[1], full), sibling).wait_recv()

    @pl.when(has_after)
    def _():
        halo(1, x_ref, rows(piece[5], full), sibling).wait_recv()

    @pl.when(has_wide)
    def _():
        wide.start()

    @pl.when(has_edge)
    def _():
        edge.start()

    def fill(missing, start, size):
        @pl.when(missing)
        def _():
            copy = pltpu.make_async_copy(zeros.at[pl.ds(0, size), :], rows(start, size), fill_sem.at[0])
            copy.start()
            copy.wait()

    fill(jnp.logical_not(has_before), piece[1], full)
    fill(jnp.logical_not(has_after), piece[5], full)
    gets_wide = jnp.where(odd == 1, has_after, has_before)
    gets_edge = jnp.where(odd == 1, has_before, has_after)
    wide_at = piece[2] + odd * (piece[4] - piece[2])
    edge_at = piece[6] * (1 - odd)
    far_at = piece[6] * odd
    own_at = piece[4] + odd * (piece[2] - piece[4])
    fill(jnp.logical_not(gets_wide), wide_at, full)
    fill(jnp.logical_not(gets_edge), edge_at, part)
    fill(jnp.logical_not(has_far), far_at, part)
    halo(3, x_ref, rows(own_at, full), sibling).wait_recv()

    @pl.when(has_far)
    def _():
        halo(2, far_rows, rows(far_at, part), sibling).wait_recv()

    @pl.when(gets_wide)
    def _():
        halo(4, x_ref, rows(wide_at, full), sibling).wait_recv()

    @pl.when(gets_edge)
    def _():
        halo(5, far_rows, rows(edge_at, part), sibling).wait_recv()

    for copy in copies:
        copy.wait_send()
    for exists, copy in ((has_after, after), (has_before, before), (has_far, far), (has_wide, wide), (has_edge, edge)):
        pl.when(exists)(copy.wait_send)
    keep_own.wait()
    for i in range(3):
        pltpu.make_async_copy(bufs[i], w_out.at[:, :, pl.ds(i * width, width)], out_sem.at[i]).wait()
    pltpu.make_async_copy(buf_v, v_out, out_sem.at[3]).wait()


def gather_weights(query, key, value, vectors, own, count):
    rows, columns = query.shape[0], 3 * query.shape[1]
    bits = count.bit_length() - 1
    vmem, any_space = pl.BlockSpec(memory_space=pltpu.VMEM), pl.BlockSpec(memory_space=pl.ANY)
    return pl.pallas_call(
        functools.partial(gather_kernel, count),
        out_shape=(
            jax.ShapeDtypeStruct((count, rows, columns), BF),
            jax.ShapeDtypeStruct((count,) + vectors.shape, BF),
            jax.ShapeDtypeStruct((own.shape[0] + 2 * REACH * BLOCK, own.shape[1]), BF),
        ),
        in_specs=[vmem] * 5,
        out_specs=[any_space, any_space, any_space],
        scratch_shapes=[pltpu.VMEM((rows, columns), BF), pltpu.VMEM(vectors.shape, BF)]
        + [pltpu.VMEM((count, rows, columns // 3), BF)] * 3
        + [
            pltpu.VMEM((count,) + vectors.shape, BF),
            pltpu.VMEM(own.shape, BF),
            pltpu.SemaphoreType.DMA((5,)),
            pltpu.SemaphoreType.DMA((4,)),
            pltpu.SemaphoreType.DMA((4, bits)),
            pltpu.SemaphoreType.DMA((4, bits)),
            pltpu.SemaphoreType.DMA((6,)),
            pltpu.SemaphoreType.DMA((6,)),
            pltpu.SemaphoreType.DMA((1,)),
        ],
        compiler_params=pltpu.CompilerParams(
            collective_id=0, has_side_effects=True, vmem_limit_bytes=60 * 1024 * 1024
        ),
        cost_estimate=pl.CostEstimate(flops=0, bytes_accessed=200_000_000, transcendentals=0),
        name="gather_weights",
    )(query, key, value, vectors, own)


def reduce_kernel(
    count, q_ref, kv_ref, v_ref, x_ref, wq_out, wk_out, wv_out, v_out, x_out, buf_a, buf_b, buf_c, got_a, got_b, got_c, sum_v, got_v,
    left, mid, right, e_own, e_wide, e_edge, e_far, from_after, from_before, load_sem, send_sem, recv_sem, halo_send,
    halo_recv,
):
    me = lax.axis_index("ctx")
    orders = link_orders(count)
    bits = len(orders[0])
    bufs, gots = [buf_a, buf_b, buf_c], [got_a, got_b, got_c]
    width = q_ref.shape[2]
    full = left.shape[0]
    part, piece = halo_sizes(full)
    odd, has_before, has_after, has_far, partner = halo_links(me, count)
    sibling = across(me, 0)

    def rows(start, size):
        return x_ref.at[pl.ds(pl.multiple_of(start, BLOCK), size), :]

    def halo(index, source, target, device):
        return remote(source, target, halo_send.at[index], halo_recv.at[index], device)

    loads = [
        pltpu.make_async_copy(rows(piece[1], full), left, load_sem.at[4]),
        pltpu.make_async_copy(rows(piece[3], full), mid, load_sem.at[5]),
        pltpu.make_async_copy(rows(piece[5], full), right, load_sem.at[6]),
    ]
    for copy in loads:
        copy.start()

    def load(j, carry):
        pltpu.make_async_copy(q_ref.at[j], bufs[0].at[place_of(j, orders[0])], load_sem.at[0]).start()
        for i in (1, 2):
            pltpu.make_async_copy(
                kv_ref.at[j, :, pl.ds((i - 1) * width, width)], bufs[i].at[place_of(j, orders[i])], load_sem.at[i]
            ).start()
        return carry

    lax.fori_loop(0, count, load, 0)
    first_sum = pltpu.make_async_copy(v_ref, sum_v.at[0], load_sem.at[3])
    first_sum.start()
    greet(me, bits, count)

    swaps = [
        halo(3, rows(piece[2] + odd * (piece[4] - piece[2]), full), e_wide, sibling),
        halo(4, rows(piece[6] * (1 - odd), part), e_edge, sibling),
        halo(5, rows(piece[4] + odd * (piece[2] - piece[4]), full), e_own, sibling),
    ]
    for copy in swaps:
        copy.start()
    far = halo(2, rows(piece[6] * odd, part), e_far, partner)

    @pl.when(has_far)
    def _():
        far.start()

    for copy in loads:
        copy.wait()
    swaps[0].wait_recv()
    swaps[1].wait_recv()

    def add_into(target, start, source, size):
        def add(j, carry):
            at = pl.ds(pl.multiple_of(start + j * BLOCK, BLOCK), BLOCK)
            total = target[at, :].astype(F32) + source[pl.ds(pl.multiple_of(j * BLOCK, BLOCK), BLOCK), :].astype(F32)
            target[at, :] = total.astype(target.dtype)
            return carry

        lax.fori_loop(0, size // BLOCK, add, 0)

    @pl.when(odd == 0)
    def _():
        add_into(left, full - part, e_edge, part)
        add_into(right, 0, e_wide, full)

    @pl.when(odd == 1)
    def _():
        add_into(left, 0, e_wide, full)
        add_into(right, 0, e_edge, part)

    before = halo(0, left, from_after, me - 2)
    after = halo(1, right, from_before, me + 2)

    @pl.when(has_before)
    def _():
        before.start()

    @pl.when(has_after)
    def _():
        after.start()

    for i in range(3):
        source = q_ref if i == 0 else kv_ref.at[:, :, pl.ds((i - 1) * width, width)]
        pltpu.make_async_copy(source, bufs[i], load_sem.at[i]).wait()
    first_sum.wait()
    places = [place_of(me, order) for order in orders]
    copies = []
    for k in range(bits):
        bit = bits - 1 - k
        half = 1 << bit
        offset = count - 2 * half
        stage = []
        for i in range(3):
            keep = (places[i] // half) * half
            give = keep + half * (1 - 2 * bit_of(places[i], bit))
            copy = remote(
                bufs[i].at[pl.ds(give, half)], gots[i].at[pl.ds(offset, half)], send_sem.at[i, k], recv_sem.at[i, k],
                across(me, orders[i][bit]),
            )
            copy.start()
            stage.append(copy)
        copy = remote(sum_v.at[k], got_v.at[k], send_sem.at[3, k], recv_sem.at[3, k], across(me, orders[0][bit]))
        copy.start()
        stage.append(copy)
        for i in range(3):
            stage[i].wait_recv()
            keep = (places[i] // half) * half
            if k == bits - 1:
                total = bufs[i][keep].astype(F32) + gots[i][offset].astype(F32)
                if i == 0:
                    wq_out[...] = total
                else:
                    for j in range(width // LANES):
                        place = ((i - 1) * width // LANES + j) // 2 * LANES
                        target = wv_out if ((i - 1) * width // LANES + j) % 2 else wk_out
                        target[:, place : place + LANES] = total[:, j * LANES : (j + 1) * LANES]
            else:

                def add(j, carry, i=i, keep=keep, offset=offset):
                    total = bufs[i][keep + j].astype(F32) + gots[i][offset + j].astype(F32)
                    bufs[i][keep + j] = total.astype(BF)
                    return carry

                lax.fori_loop(0, half, add, 0)
        stage[3].wait_recv()
        if k == bits - 1:
            v_out[...] = sum_v[k] + got_v[k]
        else:
            sum_v[k + 1] = sum_v[k] + got_v[k]
        copies += stage

    swaps[2].wait_recv()

    def start_sum(j, carry):
        at = pl.ds(pl.multiple_of(j * BLOCK, BLOCK), BLOCK)
        x_out[at, :] = mid[at, :].astype(F32) + e_own[at, :].astype(F32)
        return carry

    lax.fori_loop(0, full // BLOCK, start_sum, 0)

    @pl.when(has_far)
    def _():
        far.wait_recv()
        add_into(x_out, odd * (full - part), e_far, part)

    @pl.when(has_after)
    def _():
        before.wait_recv()
        add_into(x_out, 0, from_after, full)

    @pl.when(has_before)
    def _():
        after.wait_recv()
        add_into(x_out, 0, from_before, full)

    for copy in copies + swaps:
        copy.wait_send()
    for exists, copy in ((has_after, after), (has_before, before), (has_far, far)):
        pl.when(exists)(copy.wait_send)


def reduce_grads(query_grads, kv_grads, vectors, halo_grads, own_rows, count):
    _, rows, columns = query_grads.shape
    bits = count.bit_length() - 1
    vmem, any_space = pl.BlockSpec(memory_space=pltpu.VMEM), pl.BlockSpec(memory_space=pl.ANY)
    slabs = pltpu.VMEM((count, rows, columns), BF)
    stages = pltpu.VMEM((bits,) + vectors.shape, F32)
    part, _ = halo_sizes(own_rows)
    whole, piece = pltpu.VMEM((own_rows, columns), BF), pltpu.VMEM((part, columns), BF)
    return pl.pallas_call(
        functools.partial(reduce_kernel, count),
        out_shape=(
            jax.ShapeDtypeStruct((rows, columns), F32),
            jax.ShapeDtypeStruct((rows, columns), F32),
            jax.ShapeDtypeStruct((rows, columns), F32),
            jax.ShapeDtypeStruct(vectors.shape, F32),
            jax.ShapeDtypeStruct((own_rows, columns), F32),
        ),
        in_specs=[any_space, any_space, vmem, any_space],
        out_specs=[vmem] * 5,
        scratch_shapes=[slabs] * 6
        + [stages, stages, whole, whole, whole, whole, whole, piece, piece, whole, whole]
        + [
            pltpu.SemaphoreType.DMA((7,)),
            pltpu.SemaphoreType.DMA((4, bits)),
            pltpu.SemaphoreType.DMA((4, bits)),
            pltpu.SemaphoreType.DMA((6,)),
            pltpu.SemaphoreType.DMA((6,)),
        ],
        compiler_params=pltpu.CompilerParams(
            collective_id=1, has_side_effects=True, vmem_limit_bytes=60 * 1024 * 1024
        ),
        cost_estimate=pl.CostEstimate(flops=0, bytes_accessed=200_000_000, transcendentals=0),
        name="reduce_grads",
    )(query_grads, kv_grads, vectors, halo_grads)


def low_half():
    return lax.broadcasted_iota(jnp.int32, (BLOCK, LANES), 1) < LANES // 2


def split_pair(rows):
    half = low_half()
    zero = jnp.zeros_like(rows)
    return jnp.concatenate([jnp.where(half, rows, zero), jnp.where(half, zero, rows)], axis=0)


def join_pair(rows):
    return jnp.where(low_half(), rows[:BLOCK], rows[BLOCK:])


KEY, VALUE = slice(0, LANES), slice(LANES, 2 * LANES)


def block_at(ref, position, side):
    return ref[pl.ds(pl.multiple_of(position * BLOCK, BLOCK), BLOCK), side]


def slots_of(near_ref, rand_ref, block, pair, heads):
    shared = [near_ref[block * 8 + i] for i in range(5)]
    at = (block * heads + 2 * pair) * 3
    chosen = [(rand_ref[at + i], rand_ref[at + 3 + i]) for i in range(3)]
    return shared, chosen


def slot_rows(ref, side, shared, chosen):
    half = low_half()
    parts = [block_at(ref, i, side) for i in shared]
    parts += [jnp.where(half, block_at(ref, a, side), block_at(ref, b, side)) for a, b in chosen]
    return jnp.concatenate(parts, axis=0)


def slot_bias(near_ref, block):
    after = jnp.where(near_ref[block * 8 + 5] > 0, 0.0, masked_score).astype(F32)
    lead = jnp.where(near_ref[block * 8 + 6] > 0, 0.0, masked_score).astype(F32)
    return after, lead


def masked(scores, near_ref, block):
    after, lead = slot_bias(near_ref, block)
    return jnp.concatenate(
        [
            scores[: 2 * BLOCK],
            scores[2 * BLOCK : 3 * BLOCK] + after,
            scores[3 * BLOCK : 4 * BLOCK],
            scores[4 * BLOCK : 5 * BLOCK] + lead,
            scores[5 * BLOCK :],
        ],
        axis=0,
    )


def forward_kernel(heads, own_blocks, near_ref, rand_ref, glob_ref, q_ref, kv_ref, o_ref, s_ref):
    pair = pl.program_id(0)

    def regular(block, carry):
        rows = pl.ds(pl.multiple_of(block * BLOCK, BLOCK), BLOCK)
        shared, chosen = slots_of(near_ref, rand_ref, block, pair, heads)
        queries = split_pair(q_ref[rows, :] * 0.125)
        scores = masked(cols_dot(slot_rows(kv_ref, KEY, shared, chosen), queries), near_ref, block)
        weights = jnp.exp(scores - jnp.max(scores, axis=0, keepdims=True))
        probs = weights * (1.0 / jnp.sum(weights, axis=0, keepdims=True))
        mixed = rows_dot(probs.astype(BF), slot_rows(kv_ref, VALUE, shared, chosen))
        o_ref[rows, :] = join_pair(mixed).astype(BF)
        return carry

    lax.fori_loop(0, own_blocks, regular, 0, unroll=own_blocks)

    def whole(block, carry):
        @pl.when(glob_ref[block * 4] > 0)
        def _():
            rows = pl.ds(pl.multiple_of(block * BLOCK, BLOCK), BLOCK)
            first = glob_ref[block * 4 + 1]
            length = glob_ref[block * 4 + 2]
            queries = split_pair(q_ref[rows, :] * 0.125)
            slot_id = lax.broadcasted_iota(jnp.int32, (WIDE, LANES), 0) // BLOCK

            def score(step, top):
                at = pl.ds(pl.multiple_of((first + step * SLOTS) * BLOCK, BLOCK), WIDE)
                scores = cols_dot(kv_ref[at, KEY], queries)
                scores = jnp.where(slot_id < length - step * SLOTS, scores, masked_score)
                s_ref[step] = scores
                return jnp.maximum(top, jnp.max(scores, axis=0, keepdims=True))

            top = lax.fori_loop(0, CHUNKS, score, jnp.full((1, LANES), masked_score, F32), unroll=True)

            def mix(step, kept):
                total, acc = kept
                at = pl.ds(pl.multiple_of((first + step * SLOTS) * BLOCK, BLOCK), WIDE)
                weights = jnp.exp(s_ref[step] - top)
                return (
                    total + jnp.sum(weights, axis=0, keepdims=True),
                    acc + rows_dot(weights.astype(BF), kv_ref[at, VALUE]),
                )

            total, acc = lax.fori_loop(0, CHUNKS, mix, (jnp.zeros((1, LANES), F32), jnp.zeros((LANES, LANES), F32)), unroll=True)
            scale = jnp.transpose(jnp.broadcast_to(1.0 / total, (LANES, LANES)))
            o_ref[rows, :] = join_pair(acc * scale).astype(BF)

        return carry

    lax.fori_loop(0, own_blocks, whole, 0)


def backward_kernel(
    heads, own_blocks, near_ref, rand_ref, glob_ref, q_ref, kv_ref, c_ref,
    dq_ref, dkv_ref, sum_ref, dk_acc, dv_acc, s_ref, p_ref,
):
    pair = pl.program_id(0)
    dk_acc[...] = jnp.zeros_like(dk_acc)
    dv_acc[...] = jnp.zeros_like(dv_acc)
    half = low_half()

    def add_rows(acc, shared, chosen, update):
        for i, position in enumerate(shared):
            at = pl.ds(pl.multiple_of(position * BLOCK, BLOCK), BLOCK)
            acc[at, :] += update[i * BLOCK : (i + 1) * BLOCK]
        for i, (one, two) in enumerate(chosen):
            piece = update[(5 + i) * BLOCK : (6 + i) * BLOCK]
            at = pl.ds(pl.multiple_of(one * BLOCK, BLOCK), BLOCK)
            acc[at, :] += jnp.where(half, piece, 0.0)
            at = pl.ds(pl.multiple_of(two * BLOCK, BLOCK), BLOCK)
            acc[at, :] += jnp.where(half, 0.0, piece)

    def regular(block, carry):
        rows = pl.ds(pl.multiple_of(block * BLOCK, BLOCK), BLOCK)
        shared, chosen = slots_of(near_ref, rand_ref, block, pair, heads)
        queries = split_pair(q_ref[rows, :] * 0.125)
        slope = c_ref[rows, :]
        slope = split_pair(jnp.where(glob_ref[block * 4] > 0, jnp.zeros_like(slope), slope))
        keys = slot_rows(kv_ref, KEY, shared, chosen)
        scores = masked(cols_dot(keys, queries), near_ref, block)
        weights = jnp.exp(scores - jnp.max(scores, axis=0, keepdims=True))
        probs = weights * (1.0 / jnp.sum(weights, axis=0, keepdims=True))
        dprobs = cols_dot(slot_rows(kv_ref, VALUE, shared, chosen), slope)
        inner = jnp.sum(probs * dprobs, axis=0, keepdims=True)
        dscores = (probs * (dprobs - inner)).astype(BF)
        dq_ref[rows, :] = (join_pair(rows_dot(dscores, keys)) * 0.125).astype(BF)
        add_rows(dk_acc, shared, chosen, plain_dot(dscores, queries))
        add_rows(dv_acc, shared, chosen, plain_dot(probs.astype(BF), slope))
        return carry

    lax.fori_loop(0, own_blocks, regular, 0, unroll=6)

    def whole(block, carry):
        @pl.when(glob_ref[block * 4] > 0)
        def _():
            rows = pl.ds(pl.multiple_of(block * BLOCK, BLOCK), BLOCK)
            first = glob_ref[block * 4 + 1]
            length = glob_ref[block * 4 + 2]
            queries = split_pair(q_ref[rows, :] * 0.125)
            slope = split_pair(c_ref[rows, :])
            slot_id = lax.broadcasted_iota(jnp.int32, (WIDE, LANES), 0) // BLOCK

            def score(step, top):
                at = pl.ds(pl.multiple_of((first + step * SLOTS) * BLOCK, BLOCK), WIDE)
                scores = cols_dot(kv_ref[at, KEY], queries)
                scores = jnp.where(slot_id < length - step * SLOTS, scores, masked_score)
                s_ref[step] = scores
                p_ref[step] = cols_dot(kv_ref[at, VALUE], slope)
                return jnp.maximum(top, jnp.max(scores, axis=0, keepdims=True))

            top = lax.fori_loop(0, CHUNKS, score, jnp.full((1, LANES), masked_score, F32), unroll=True)

            def weigh(step, kept):
                total, inner = kept
                weights = jnp.exp(s_ref[step] - top)
                s_ref[step] = weights
                return (
                    total + jnp.sum(weights, axis=0, keepdims=True),
                    inner + jnp.sum(weights * p_ref[step], axis=0, keepdims=True),
                )

            zero_row = jnp.zeros((1, LANES), F32)
            total, inner = lax.fori_loop(0, CHUNKS, weigh, (zero_row, zero_row), unroll=True)
            scale = 1.0 / total
            inner = inner * scale

            def spread(step, dq_sum):
                at = pl.ds(pl.multiple_of((first + step * SLOTS) * BLOCK, BLOCK), WIDE)
                probs = s_ref[step] * scale
                dscores = (probs * (p_ref[step] - inner)).astype(BF)
                dk_acc[at, :] += plain_dot(dscores, queries)
                dv_acc[at, :] += plain_dot(probs.astype(BF), slope)
                return dq_sum + rows_dot(dscores, kv_ref[at, KEY])

            dq_sum = lax.fori_loop(0, CHUNKS, spread, jnp.zeros((LANES, LANES), F32), unroll=True)
            dq_ref[rows, :] = (join_pair(dq_sum) * 0.125).astype(BF)

        return carry

    lax.fori_loop(0, own_blocks, whole, 0)
    dkv_ref[:, KEY] = dk_acc[...].astype(BF)
    dv_low = dv_acc[...].astype(BF)
    dkv_ref[:, VALUE] = dv_low
    sum_ref[0:1, :] = jnp.sum(dq_ref[...].astype(F32), axis=0, keepdims=True)
    sum_ref[1:2, :] = jnp.sum(dv_low.astype(F32), axis=0, keepdims=True)


def attention_calls(row_count, model_width, heads, buf_rows):
    own_blocks = row_count // BLOCK
    pairs = heads // 2
    own = lambda: pl.BlockSpec((row_count, LANES), lambda p, *_: (0, p))
    both = lambda: pl.BlockSpec((buf_rows, 2 * LANES), lambda p, *_: (0, p))
    params = lambda: pltpu.CompilerParams(vmem_limit_bytes=48 * 1024 * 1024)
    forward = pl.pallas_call(
        functools.partial(forward_kernel, heads, own_blocks),
        out_shape=jax.ShapeDtypeStruct((row_count, model_width), BF),
        grid_spec=pltpu.PrefetchScalarGridSpec(
            num_scalar_prefetch=3,
            grid=(pairs,),
            in_specs=[own(), both()],
            out_specs=own(),
            scratch_shapes=[pltpu.VMEM((CHUNKS, WIDE, LANES), F32)],
        ),
        compiler_params=params(),
        cost_estimate=pl.CostEstimate(
            flops=4 * row_count * WIDE * 2 * model_width, bytes_accessed=4 * buf_rows * model_width,
            transcendentals=row_count * WIDE * heads,
        ),
        name="attend_forward",
    )
    backward = pl.pallas_call(
        functools.partial(backward_kernel, heads, own_blocks),
        out_shape=(
            jax.ShapeDtypeStruct((row_count, model_width), BF),
            jax.ShapeDtypeStruct((buf_rows, 2 * model_width), BF),
            jax.ShapeDtypeStruct((2, model_width), F32),
        ),
        grid_spec=pltpu.PrefetchScalarGridSpec(
            num_scalar_prefetch=3,
            grid=(pairs,),
            in_specs=[own(), both(), own()],
            out_specs=[own(), both(), pl.BlockSpec((2, LANES), lambda p, *_: (0, p))],
            scratch_shapes=[
                pltpu.VMEM((buf_rows, LANES), F32),
                pltpu.VMEM((buf_rows, LANES), F32),
                pltpu.VMEM((CHUNKS, WIDE, LANES), F32),
                pltpu.VMEM((CHUNKS, WIDE, LANES), F32),
            ],
        ),
        compiler_params=params(),
        cost_estimate=pl.CostEstimate(
            flops=10 * row_count * WIDE * 2 * model_width, bytes_accessed=8 * buf_rows * model_width,
            transcendentals=row_count * WIDE * heads,
        ),
        name="attend_backward",
    )
    return forward, backward


def interleaved(one, two):
    return jnp.concatenate(
        [side[..., i : i + LANES] for i in range(0, one.shape[-1], LANES) for side in (one, two)], axis=-1
    )


def on_device(
    layer_input, out_grad, doc_starts, rand_blocks, query_weight, query_bias, key_weight, value_weight,
    value_bias, output_weight, output_bias, first_gain, first_shift, inner_weight, inner_bias,
    outer_weight, outer_bias, second_gain, second_shift,
):
    row_count, model_width = layer_input.shape
    head_count = rand_blocks.shape[1]
    devices = lax.axis_size("ctx")
    own_blocks = row_count // BLOCK
    buf_blocks = 2 * REACH + own_blocks
    own_first = lax.axis_index("ctx") * own_blocks
    buf_first = own_first - REACH
    block_total = own_blocks * devices
    own_ids = own_first + jnp.arange(own_blocks, dtype=jnp.int32)
    own_doc, own_start = doc_layout(doc_starts, own_ids)
    next_doc = doc_layout(doc_starts, own_ids + 1)[0]
    start_blocks = doc_starts // BLOCK
    later = start_blocks[None, :] > own_ids[:, None]
    doc_end = jnp.min(jnp.where(later, start_blocks[None, :], block_total), axis=1)
    glob_own = own_ids - own_start < 2

    def local(ids):
        return jnp.clip(ids - buf_first, 0, buf_blocks - 1).astype(jnp.int32)

    near = jnp.stack(
        [
            local(own_ids - 1),
            local(own_ids),
            local(own_ids + 1),
            local(own_start),
            local(own_start + 1),
            ((own_ids + 1 < block_total) & (next_doc == own_doc)).astype(jnp.int32),
            (own_ids - own_start > 2).astype(jnp.int32),
            jnp.zeros_like(own_ids),
        ],
        axis=1,
    ).reshape(-1)
    picks = local(rand_blocks).reshape(-1)
    spans = jnp.stack(
        [glob_own.astype(jnp.int32), local(own_start), doc_end - own_start, jnp.zeros_like(own_ids)], axis=1
    ).reshape(-1)
    attend, attend_back = attention_calls(row_count, model_width, head_count, buf_blocks * BLOCK)
    m = model_width
    unit = query_bias.shape[0]
    weight_rows = query_weight.shape[0]

    def gathered(value):
        return lax.all_gather(value, "ctx", axis=0, tiled=True)

    vectors = jnp.concatenate(
        [
            query_bias, value_bias, output_bias, first_gain, first_shift, outer_bias, second_gain, second_shift,
            inner_bias,
        ]
    )
    lane_pad = -vectors.shape[0] % LANES
    first_all, vector_all, x_buf = gather_weights(
        query_weight, key_weight, value_weight, jnp.pad(vectors, (0, lane_pad))[None, :], layer_input, devices
    )
    w_qkv = first_all.reshape(m, 3 * m)
    vector_all = vector_all[:, 0].astype(F32)
    b_query, b_value, b_output, g_first, s_first, b_outer, g_second, s_second = [
        vector_all[:, i * unit : (i + 1) * unit].reshape(-1) for i in range(8)
    ]
    b_inner = vector_all[:, 8 * unit : 8 * unit + inner_bias.shape[0]].reshape(-1)
    outer_rows = outer_weight.shape[0]
    hidden_blocks = inner_weight.shape[1] // m
    late = gathered(
        jnp.concatenate(
            [outer_weight, output_weight] + [inner_weight[:, i * m : (i + 1) * m] for i in range(hidden_blocks)], axis=0
        ).astype(BF)[None]
    )
    w_outer = late[:, :outer_rows].reshape(-1, m)
    w_output, *w_inner = [
        late[:, outer_rows + i * weight_rows : outer_rows + (i + 1) * weight_rows].reshape(m, m)
        for i in range(1 + hidden_blocks)
    ]
    w_inner = jnp.concatenate(w_inner, axis=1)
    w_query, w_kv = w_qkv[:, :m], w_qkv[:, m:]

    query_rows = (plain_dot(layer_input, w_query) + b_query).astype(BF)
    kv_buf = (plain_dot(x_buf, w_kv) + interleaved(jnp.zeros_like(b_value), b_value)).astype(BF)
    context_rows = attend(near, picks, spans, query_rows, kv_buf)

    input_float = layer_input.astype(F32)
    resid_one = input_float + plain_dot(context_rows, w_output) + b_output
    normed_one, first_pull = jax.vjp(layer_norm, resid_one, g_first, s_first)
    normed_low = normed_one.astype(BF)
    inner_pre = plain_dot(normed_low, w_inner) + b_inner
    active, active_slope = gelu_and_slope(inner_pre)
    active, active_slope = lax.optimization_barrier((active.astype(BF), active_slope))
    resid_two = normed_one + plain_dot(active, w_outer) + b_outer
    normed_two, second_pull = jax.vjp(layer_norm, resid_two, g_second, s_second)
    layer_out = normed_two.astype(BF)

    def scattered(value):
        return lax.psum_scatter(value, "ctx", scatter_dimension=0, tiled=True).astype(F32)

    grad_two, grad_second_gain, grad_second_shift = second_pull(out_grad.astype(F32))
    grad_two_low = grad_two.astype(BF)
    grad_outer_bias = jnp.sum(grad_two_low.astype(F32), axis=0)
    grad_outer_weight = rows_dot(active, grad_two_low).astype(BF)
    grad_inner = (cols_dot(grad_two_low, w_outer) * active_slope).astype(BF)
    grad_inner_bias = jnp.sum(grad_inner.astype(F32), axis=0)
    grad_inner_weight = rows_dot(normed_low, grad_inner).astype(BF)
    grad_one = grad_two + cols_dot(grad_inner, w_inner)
    grad_resid_one, grad_first_gain, grad_first_shift = first_pull(grad_one)
    grad_one_low = grad_resid_one.astype(BF)
    grad_output_bias = jnp.sum(grad_one_low.astype(F32), axis=0)
    grad_output_weight = rows_dot(context_rows, grad_one_low).astype(BF)
    slabs = lambda value: value.reshape(devices, -1, m)
    late_grads = scattered(
        jnp.concatenate(
            [slabs(grad_outer_weight), slabs(grad_output_weight)]
            + [slabs(grad_inner_weight[:, i * m : (i + 1) * m]) for i in range(hidden_blocks)],
            axis=1,
        )
    )[0]
    grad_outer_weight = late_grads[:outer_rows]
    late_grads = late_grads[outer_rows:].reshape(1 + hidden_blocks, weight_rows, m)
    grad_output_weight = late_grads[0]
    grad_inner_weight = jnp.concatenate([late_grads[1 + i] for i in range(hidden_blocks)], axis=1)
    context_gradient = cols_dot(grad_one_low, w_output).astype(BF)

    query_low, kv_low, attn_sums = attend_back(near, picks, spans, query_rows, kv_buf, context_gradient)
    grad_x_buf = cols_dot(kv_low, w_kv).astype(BF)
    grad_vectors = jnp.concatenate(
        [
            attn_sums,
            jnp.stack(
                [
                    grad_output_bias, grad_first_gain, grad_first_shift, grad_outer_bias, grad_second_gain,
                    grad_second_shift,
                ]
            ),
            grad_inner_bias.reshape(-1, m),
        ],
        axis=0,
    )
    grad_query_weight, grad_key_weight, grad_value_weight, sums, halo_part = reduce_grads(
        rows_dot(layer_input, query_low).astype(BF).reshape(devices, -1, m),
        rows_dot(x_buf, kv_low).astype(BF).reshape(devices, -1, 2 * m),
        grad_vectors,
        grad_x_buf,
        row_count,
        devices,
    )
    grad_input = grad_resid_one + cols_dot(query_low, w_query) + halo_part
    me = lax.axis_index("ctx")
    own_sums = lax.dynamic_slice_in_dim(sums[:8], me * unit, unit, 1)
    v_query, v_value, v_output, v_gain1, v_shift1, v_outer, v_gain2, v_shift2 = [own_sums[i] for i in range(8)]
    inner_unit = inner_bias.shape[0]
    inner_at = me * inner_unit
    v_inner = lax.dynamic_slice(sums, (8 + inner_at // m, inner_at % m), (1, inner_unit))[0]
    return (
        layer_out, grad_input, grad_query_weight, v_query, grad_key_weight, grad_value_weight, v_value,
        grad_output_weight, v_output, v_gain1, v_shift1, grad_inner_weight, v_inner, grad_outer_weight, v_outer,
        v_gain2, v_shift2,
    )


def solution(mesh):
    rows, line = P("ctx", None), P("ctx")
    in_specs = (
        rows, rows, P(), P("ctx", None, None), rows, line, rows, rows, line, rows, line, line, line, rows, line, rows,
        line, line, line,
    )
    out_specs = (
        rows, rows, rows, line, rows, rows, line, rows, line, line, line, rows, line, rows, line, line, line,
    )
    return jax.shard_map(on_device, mesh=mesh, in_specs=in_specs, out_specs=out_specs, check_vma=False)
```

```python
import functools
import math

import jax
import jax.numpy as jnp
from jax import lax
from jax.experimental import pallas as pl
from jax.experimental.pallas import tpu as pltpu
from jax.sharding import PartitionSpec as P

BLOCK = 64
DOC_MAX = 32
REACH = DOC_MAX - 1
SLOTS = 8
WIDE = SLOTS * BLOCK
CHUNKS = DOC_MAX // SLOTS
LANES = 128

norm_eps = 1e-06
masked_score = -1e30
BF = jnp.bfloat16
F32 = jnp.float32


def layer_norm(hidden, scale_gain, shift_vec):
    row_mean = jnp.mean(hidden, axis=-1, keepdims=True)
    centred = hidden - row_mean
    variance = jnp.mean(centred * centred, axis=-1, keepdims=True)
    return centred * lax.rsqrt(variance + norm_eps) * scale_gain + shift_vec


def gelu_and_slope(inner_pre):
    below = 0.5 + 0.5 * lax.erf(inner_pre * math.sqrt(0.5))
    density = jnp.exp(-0.5 * inner_pre * inner_pre) * (1.0 / math.sqrt(2.0 * math.pi))
    return (inner_pre * below, below + inner_pre * density)


def plain_dot(left, right):
    return jnp.dot(left, right, preferred_element_type=F32)


def rows_dot(left, right):
    return lax.dot_general(left, right, (((0,), (0,)), ((), ())), preferred_element_type=F32)


def cols_dot(left, right):
    return lax.dot_general(left, right, (((1,), (1,)), ((), ())), preferred_element_type=F32)


def doc_layout(doc_starts, block_ids):
    start_blocks = doc_starts // BLOCK
    before = start_blocks[None, :] <= block_ids[:, None]
    doc_ids = jnp.sum(before.astype(jnp.int32), axis=1) - 1
    first_block = jnp.max(jnp.where(before, start_blocks[None, :], -1), axis=1)
    return (doc_ids, first_block)


def link_orders(count):
    bits = count.bit_length() - 1
    assert count == 1 << bits and bits >= 4, count
    high = list(range(bits - 1, 2, -1))
    return [[1] + high + [2, 0], [1, 2] + high + [0], [1] + high[:-1] + [2] + high[-1:] + [0]]


def bit_of(index, bit):
    return (index // (1 << bit)) % 2


def across(index, bit):
    return index + (1 << bit) * (1 - 2 * bit_of(index, bit))


def place_of(index, order):
    return sum(bit_of(index, bit) * (1 << k) for k, bit in enumerate(order))


def remote(source, target, send_sem, recv_sem, device):
    return pltpu.make_async_remote_copy(
        src_ref=source, dst_ref=target, send_sem=send_sem, recv_sem=recv_sem, device_id=(device,),
        device_id_type=pl.DeviceIdType.MESH,
    )


def halo_sizes(own_rows):
    far = REACH * BLOCK - 2 * own_rows
    assert 0 < far <= own_rows, own_rows
    return far, [0] + [far + own_rows * i for i in range(6)]


def halo_links(me, count):
    odd = me % 2
    partner = me - 3 + 6 * odd
    return odd, me >= 2, me < count - 2, (partner >= 0) & (partner < count), partner


def greet(me, bits, count):
    barrier = pltpu.get_barrier_semaphore()

    def hello(device):
        pl.semaphore_signal(barrier, inc=1, device_id=(device,), device_id_type=pl.DeviceIdType.MESH)

    _, has_before, has_after, has_far, partner = halo_links(me, count)
    for bit in range(bits):
        hello(across(me, bit))

    @pl.when(has_before)
    def _():
        hello(me - 2)

    @pl.when(has_after)
    def _():
        hello(me + 2)

    @pl.when(has_far)
    def _():
        hello(partner)

    expected = bits + has_before.astype(jnp.int32) + has_after.astype(jnp.int32) + has_far.astype(jnp.int32)
    pl.semaphore_wait(barrier, expected)


def gather_kernel(
    count, wq_ref, wk_ref, wv_ref, v_ref, x_ref, w_out, v_out, x_out, low_w, low_v, buf_a, buf_b, buf_c, buf_v, zeros, local_sem, out_sem, send_sem,
    recv_sem, halo_send, halo_recv, fill_sem,
):
    me = lax.axis_index("ctx")
    orders = link_orders(count)
    bits = len(orders[0])
    width = wq_ref.shape[1]
    low_w[:, :width] = wq_ref[...].astype(BF)
    for i in range(width // LANES):
        start = width + 2 * i * LANES
        low_w[:, start : start + LANES] = wk_ref[:, i * LANES : (i + 1) * LANES].astype(BF)
        low_w[:, start + LANES : start + 2 * LANES] = wv_ref[:, i * LANES : (i + 1) * LANES].astype(BF)
    low_v[...] = v_ref[...].astype(BF)
    orders = orders + [orders[0]]
    bufs = [buf_a, buf_b, buf_c, buf_v]
    sources = [low_w.at[:, pl.ds(i * width, width)] for i in range(3)] + [low_v]
    places = [place_of(me, order) for order in orders]
    full = x_ref.shape[0]
    part, piece = halo_sizes(full)
    odd, has_before, has_after, has_far, partner = halo_links(me, count)
    sibling = across(me, 0)

    def rows(start, size):
        return x_out.at[pl.ds(pl.multiple_of(start, BLOCK), size), :]

    def halo(index, source, target, device):
        return remote(source, target, halo_send.at[index], halo_recv.at[index], device)

    zeros[...] = jnp.zeros_like(zeros)
    keep_own = pltpu.make_async_copy(x_ref, rows(piece[3], full), local_sem.at[4])
    keep_own.start()
    greet(me, bits, count)
    for i in range(4):
        pltpu.make_async_copy(sources[i], bufs[i].at[places[i]], local_sem.at[i]).start()

    after = halo(0, x_ref, rows(piece[1], full), me + 2)
    before = halo(1, x_ref, rows(piece[5], full), me - 2)
    far_rows = x_ref.at[pl.ds(pl.multiple_of(odd * (full - part), BLOCK), part), :]
    far = halo(2, far_rows, rows((1 - odd) * piece[6], part), partner)
    own = halo(3, x_ref, rows(piece[2] + odd * (piece[4] - piece[2]), full), sibling)
    wide = halo(
        4, rows(piece[5] + odd * (piece[1] - piece[5]), full), rows(piece[4] + odd * (piece[2] - piece[4]), full), sibling
    )
    edge_from = (piece[1] + full - part) * (1 - odd) + piece[5] * odd
    edge = halo(5, rows(edge_from, part), rows(piece[6] * odd, part), sibling)
    has_wide = jnp.where(odd == 1, has_before, has_after)
    has_edge = jnp.where(odd == 1, has_after, has_before)

    for i in range(4):
        pltpu.make_async_copy(sources[i], bufs[i].at[places[i]], local_sem.at[i]).wait()
    copies = [own]
    for k in range(bits):
        stage = []
        for i in range(4):
            held = bufs[i].at[pl.ds((places[i] // (1 << k)) * (1 << k), 1 << k)]
            copy = remote(held, held, send_sem.at[i, k], recv_sem.at[i, k], across(me, orders[i][k]))
            copy.start()
            stage.append(copy)
        for copy in stage:
            copy.wait_recv()
        copies += stage
        if k == 0:
            own.start()
            pl.when(has_after)(after.start)
            pl.when(has_before)(before.start)
            pl.when(has_far)(far.start)

    def put(j, carry):
        for i in range(3):
            pltpu.make_async_copy(
                bufs[i].at[place_of(j, orders[i])], w_out.at[j, :, pl.ds(i * width, width)], out_sem.at[i]
            ).start()
        pltpu.make_async_copy(buf_v.at[place_of(j, orders[3])], v_out.at[j], out_sem.at[3]).start()
        return carry

    lax.fori_loop(0, count, put, 0)

    @pl.when(has_before)
    def _():
        halo(0, x_ref, rows(piece[1], full), sibling).wait_recv()

    @pl.when(has_after)
    def _():
        halo(1, x_ref, rows(piece[5], full), sibling).wait_recv()

    @pl.when(has_wide)
    def _():
        wide.start()

    @pl.when(has_edge)
    def _():
        edge.start()

    def fill(missing, start, size):
        @pl.when(missing)
        def _():
            copy = pltpu.make_async_copy(zeros.at[pl.ds(0, size), :], rows(start, size), fill_sem.at[0])
            copy.start()
            copy.wait()

    fill(jnp.logical_not(has_before), piece[1], full)
    fill(jnp.logical_not(has_after), piece[5], full)
    gets_wide = jnp.where(odd == 1, has_after, has_before)
    gets_edge = jnp.where(odd == 1, has_before, has_after)
    wide_at = piece[2] + odd * (piece[4] - piece[2])
    edge_at = piece[6] * (1 - odd)
    far_at = piece[6] * odd
    own_at = piece[4] + odd * (piece[2] - piece[4])
    fill(jnp.logical_not(gets_wide), wide_at, full)
    fill(jnp.logical_not(gets_edge), edge_at, part)
    fill(jnp.logical_not(has_far), far_at, part)
    halo(3, x_ref, rows(own_at, full), sibling).wait_recv()

    @pl.when(has_far)
    def _():
        halo(2, far_rows, rows(far_at, part), sibling).wait_recv()

    @pl.when(gets_wide)
    def _():
        halo(4, x_ref, rows(wide_at, full), sibling).wait_recv()

    @pl.when(gets_edge)
    def _():
        halo(5, far_rows, rows(edge_at, part), sibling).wait_recv()

    for copy in copies:
        copy.wait_send()
    for exists, copy in ((has_after, after), (has_before, before), (has_far, far), (has_wide, wide), (has_edge, edge)):
        pl.when(exists)(copy.wait_send)
    keep_own.wait()
    for i in range(3):
        pltpu.make_async_copy(bufs[i], w_out.at[:, :, pl.ds(i * width, width)], out_sem.at[i]).wait()
    pltpu.make_async_copy(buf_v, v_out, out_sem.at[3]).wait()


def gather_weights(query, key, value, vectors, own, count):
    rows, columns = query.shape[0], 3 * query.shape[1]
    bits = count.bit_length() - 1
    vmem, any_space = pl.BlockSpec(memory_space=pltpu.VMEM), pl.BlockSpec(memory_space=pl.ANY)
    return pl.pallas_call(
        functools.partial(gather_kernel, count),
        out_shape=(
            jax.ShapeDtypeStruct((count, rows, columns), BF),
            jax.ShapeDtypeStruct((count,) + vectors.shape, BF),
            jax.ShapeDtypeStruct((own.shape[0] + 2 * REACH * BLOCK, own.shape[1]), BF),
        ),
        in_specs=[vmem] * 5,
        out_specs=[any_space, any_space, any_space],
        scratch_shapes=[pltpu.VMEM((rows, columns), BF), pltpu.VMEM(vectors.shape, BF)]
        + [pltpu.VMEM((count, rows, columns // 3), BF)] * 3
        + [
            pltpu.VMEM((count,) + vectors.shape, BF),
            pltpu.VMEM(own.shape, BF),
            pltpu.SemaphoreType.DMA((5,)),
            pltpu.SemaphoreType.DMA((4,)),
            pltpu.SemaphoreType.DMA((4, bits)),
            pltpu.SemaphoreType.DMA((4, bits)),
            pltpu.SemaphoreType.DMA((6,)),
            pltpu.SemaphoreType.DMA((6,)),
            pltpu.SemaphoreType.DMA((1,)),
        ],
        compiler_params=pltpu.CompilerParams(
            collective_id=0, has_side_effects=True, vmem_limit_bytes=60 * 1024 * 1024
        ),
        cost_estimate=pl.CostEstimate(flops=0, bytes_accessed=200_000_000, transcendentals=0),
        name="gather_weights",
    )(query, key, value, vectors, own)


def reduce_kernel(
    count, q_ref, kv_ref, v_ref, x_ref, wq_out, wk_out, wv_out, v_out, x_out, buf_a, buf_b, buf_c, got_a, got_b, got_c, sum_v, got_v,
    left, mid, right, e_own, e_wide, e_edge, e_far, from_after, from_before, load_sem, send_sem, recv_sem, halo_send,
    halo_recv,
):
    me = lax.axis_index("ctx")
    orders = link_orders(count)
    bits = len(orders[0])
    bufs, gots = [buf_a, buf_b, buf_c], [got_a, got_b, got_c]
    width = q_ref.shape[2]
    full = left.shape[0]
    part, piece = halo_sizes(full)
    odd, has_before, has_after, has_far, partner = halo_links(me, count)
    sibling = across(me, 0)

    def rows(start, size):
        return x_ref.at[pl.ds(pl.multiple_of(start, BLOCK), size), :]

    def halo(index, source, target, device):
        return remote(source, target, halo_send.at[index], halo_recv.at[index], device)

    loads = [
        pltpu.make_async_copy(rows(piece[1], full), left, load_sem.at[4]),
        pltpu.make_async_copy(rows(piece[3], full), mid, load_sem.at[5]),
        pltpu.make_async_copy(rows(piece[5], full), right, load_sem.at[6]),
    ]
    for copy in loads:
        copy.start()

    def load(j, carry):
        pltpu.make_async_copy(q_ref.at[j], bufs[0].at[place_of(j, orders[0])], load_sem.at[0]).start()
        for i in (1, 2):
            pltpu.make_async_copy(
                kv_ref.at[j, :, pl.ds((i - 1) * width, width)], bufs[i].at[place_of(j, orders[i])], load_sem.at[i]
            ).start()
        return carry

    lax.fori_loop(0, count, load, 0)
    first_sum = pltpu.make_async_copy(v_ref, sum_v.at[0], load_sem.at[3])
    first_sum.start()
    greet(me, bits, count)

    swaps = [
        halo(3, rows(piece[2] + odd * (piece[4] - piece[2]), full), e_wide, sibling),
        halo(4, rows(piece[6] * (1 - odd), part), e_edge, sibling),
        halo(5, rows(piece[4] + odd * (piece[2] - piece[4]), full), e_own, sibling),
    ]
    for copy in swaps:
        copy.start()
    far = halo(2, rows(piece[6] * odd, part), e_far, partner)

    @pl.when(has_far)
    def _():
        far.start()

    for copy in loads:
        copy.wait()
    swaps[0].wait_recv()
    swaps[1].wait_recv()

    def add_into(target, start, source, size):
        def add(j, carry):
            at = pl.ds(pl.multiple_of(start + j * BLOCK, BLOCK), BLOCK)
            total = target[at, :].astype(F32) + source[pl.ds(pl.multiple_of(j * BLOCK, BLOCK), BLOCK), :].astype(F32)
            target[at, :] = total.astype(target.dtype)
            return carry

        lax.fori_loop(0, size // BLOCK, add, 0)

    @pl.when(odd == 0)
    def _():
        add_into(left, full - part, e_edge, part)
        add_into(right, 0, e_wide, full)

    @pl.when(odd == 1)
    def _():
        add_into(left, 0, e_wide, full)
        add_into(right, 0, e_edge, part)

    before = halo(0, left, from_after, me - 2)
    after = halo(1, right, from_before, me + 2)

    @pl.when(has_before)
    def _():
        before.start()

    @pl.when(has_after)
    def _():
        after.start()

    for i in range(3):
        source = q_ref if i == 0 else kv_ref.at[:, :, pl.ds((i - 1) * width, width)]
        pltpu.make_async_copy(source, bufs[i], load_sem.at[i]).wait()
    first_sum.wait()
    places = [place_of(me, order) for order in orders]
    copies = []
    for k in range(bits):
        bit = bits - 1 - k
        half = 1 << bit
        offset = count - 2 * half
        stage = []
        for i in range(3):
            keep = (places[i] // half) * half
            give = keep + half * (1 - 2 * bit_of(places[i], bit))
            copy = remote(
                bufs[i].at[pl.ds(give, half)], gots[i].at[pl.ds(offset, half)], send_sem.at[i, k], recv_sem.at[i, k],
                across(me, orders[i][bit]),
            )
            copy.start()
            stage.append(copy)
        copy = remote(sum_v.at[k], got_v.at[k], send_sem.at[3, k], recv_sem.at[3, k], across(me, orders[0][bit]))
        copy.start()
        stage.append(copy)
        for i in range(3):
            stage[i].wait_recv()
            keep = (places[i] // half) * half
            if k == bits - 1:
                total = bufs[i][keep].astype(F32) + gots[i][offset].astype(F32)
                if i == 0:
                    wq_out[...] = total
                else:
                    for j in range(width // LANES):
                        place = ((i - 1) * width // LANES + j) // 2 * LANES
                        target = wv_out if ((i - 1) * width // LANES + j) % 2 else wk_out
                        target[:, place : place + LANES] = total[:, j * LANES : (j + 1) * LANES]
            else:

                def add(j, carry, i=i, keep=keep, offset=offset):
                    total = bufs[i][keep + j].astype(F32) + gots[i][offset + j].astype(F32)
                    bufs[i][keep + j] = total.astype(BF)
                    return carry

                lax.fori_loop(0, half, add, 0)
        stage[3].wait_recv()
        if k == bits - 1:
            v_out[...] = sum_v[k] + got_v[k]
        else:
            sum_v[k + 1] = sum_v[k] + got_v[k]
        copies += stage

    swaps[2].wait_recv()

    def start_sum(j, carry):
        at = pl.ds(pl.multiple_of(j * BLOCK, BLOCK), BLOCK)
        x_out[at, :] = mid[at, :].astype(F32) + e_own[at, :].astype(F32)
        return carry

    lax.fori_loop(0, full // BLOCK, start_sum, 0)

    @pl.when(has_far)
    def _():
        far.wait_recv()
        add_into(x_out, odd * (full - part), e_far, part)

    @pl.when(has_after)
    def _():
        before.wait_recv()
        add_into(x_out, 0, from_after, full)

    @pl.when(has_before)
    def _():
        after.wait_recv()
        add_into(x_out, 0, from_before, full)

    for copy in copies + swaps:
        copy.wait_send()
    for exists, copy in ((has_after, after), (has_before, before), (has_far, far)):
        pl.when(exists)(copy.wait_send)


def reduce_grads(query_grads, kv_grads, vectors, halo_grads, own_rows, count):
    _, rows, columns = query_grads.shape
    bits = count.bit_length() - 1
    vmem, any_space = pl.BlockSpec(memory_space=pltpu.VMEM), pl.BlockSpec(memory_space=pl.ANY)
    slabs = pltpu.VMEM((count, rows, columns), BF)
    stages = pltpu.VMEM((bits,) + vectors.shape, F32)
    part, _ = halo_sizes(own_rows)
    whole, piece = pltpu.VMEM((own_rows, columns), BF), pltpu.VMEM((part, columns), BF)
    return pl.pallas_call(
        functools.partial(reduce_kernel, count),
        out_shape=(
            jax.ShapeDtypeStruct((rows, columns), F32),
            jax.ShapeDtypeStruct((rows, columns), F32),
            jax.ShapeDtypeStruct((rows, columns), F32),
            jax.ShapeDtypeStruct(vectors.shape, F32),
            jax.ShapeDtypeStruct((own_rows, columns), F32),
        ),
        in_specs=[any_space, any_space, vmem, any_space],
        out_specs=[vmem] * 5,
        scratch_shapes=[slabs] * 6
        + [stages, stages, whole, whole, whole, whole, whole, piece, piece, whole, whole]
        + [
            pltpu.SemaphoreType.DMA((7,)),
            pltpu.SemaphoreType.DMA((4, bits)),
            pltpu.SemaphoreType.DMA((4, bits)),
            pltpu.SemaphoreType.DMA((6,)),
            pltpu.SemaphoreType.DMA((6,)),
        ],
        compiler_params=pltpu.CompilerParams(
            collective_id=1, has_side_effects=True, vmem_limit_bytes=60 * 1024 * 1024
        ),
        cost_estimate=pl.CostEstimate(flops=0, bytes_accessed=200_000_000, transcendentals=0),
        name="reduce_grads",
    )(query_grads, kv_grads, vectors, halo_grads)


def low_half():
    return lax.broadcasted_iota(jnp.int32, (BLOCK, LANES), 1) < LANES // 2


def split_pair(rows):
    half = low_half()
    zero = jnp.zeros_like(rows)
    return jnp.concatenate([jnp.where(half, rows, zero), jnp.where(half, zero, rows)], axis=0)


def join_pair(rows):
    return jnp.where(low_half(), rows[:BLOCK], rows[BLOCK:])


KEY, VALUE = slice(0, LANES), slice(LANES, 2 * LANES)


def block_at(ref, position, side):
    return ref[pl.ds(pl.multiple_of(position * BLOCK, BLOCK), BLOCK), side]


def slots_of(near_ref, rand_ref, block, pair, heads):
    shared = [near_ref[block * 8 + i] for i in range(5)]
    at = (block * heads + 2 * pair) * 3
    chosen = [(rand_ref[at + i], rand_ref[at + 3 + i]) for i in range(3)]
    return shared, chosen


def slot_rows(ref, side, shared, chosen):
    half = low_half()
    parts = [block_at(ref, i, side) for i in shared]
    parts += [jnp.where(half, block_at(ref, a, side), block_at(ref, b, side)) for a, b in chosen]
    return jnp.concatenate(parts, axis=0)


def slot_bias(near_ref, block):
    after = jnp.where(near_ref[block * 8 + 5] > 0, 0.0, masked_score).astype(F32)
    lead = jnp.where(near_ref[block * 8 + 6] > 0, 0.0, masked_score).astype(F32)
    return after, lead


def masked(scores, near_ref, block):
    after, lead = slot_bias(near_ref, block)
    return jnp.concatenate(
        [
            scores[: 2 * BLOCK],
            scores[2 * BLOCK : 3 * BLOCK] + after,
            scores[3 * BLOCK : 4 * BLOCK],
            scores[4 * BLOCK : 5 * BLOCK] + lead,
            scores[5 * BLOCK :],
        ],
        axis=0,
    )


def forward_kernel(heads, own_blocks, near_ref, rand_ref, glob_ref, q_ref, kv_ref, o_ref, s_ref):
    pair = pl.program_id(0)

    def regular(block, carry):
        rows = pl.ds(pl.multiple_of(block * BLOCK, BLOCK), BLOCK)
        shared, chosen = slots_of(near_ref, rand_ref, block, pair, heads)
        queries = split_pair(q_ref[rows, :] * 0.125)
        scores = masked(cols_dot(slot_rows(kv_ref, KEY, shared, chosen), queries), near_ref, block)
        weights = jnp.exp(scores - jnp.max(scores, axis=0, keepdims=True))
        probs = weights * (1.0 / jnp.sum(weights, axis=0, keepdims=True))
        mixed = rows_dot(probs.astype(BF), slot_rows(kv_ref, VALUE, shared, chosen))
        o_ref[rows, :] = join_pair(mixed).astype(BF)
        return carry

    lax.fori_loop(0, own_blocks, regular, 0, unroll=own_blocks)

    def whole(block, carry):
        @pl.when(glob_ref[block * 4] > 0)
        def _():
            rows = pl.ds(pl.multiple_of(block * BLOCK, BLOCK), BLOCK)
            first = glob_ref[block * 4 + 1]
            length = glob_ref[block * 4 + 2]
            queries = split_pair(q_ref[rows, :] * 0.125)
            slot_id = lax.broadcasted_iota(jnp.int32, (WIDE, LANES), 0) // BLOCK

            def score(step, top):
                at = pl.ds(pl.multiple_of((first + step * SLOTS) * BLOCK, BLOCK), WIDE)
                scores = cols_dot(kv_ref[at, KEY], queries)
                scores = jnp.where(slot_id < length - step * SLOTS, scores, masked_score)
                s_ref[step] = scores
                return jnp.maximum(top, jnp.max(scores, axis=0, keepdims=True))

            top = lax.fori_loop(0, CHUNKS, score, jnp.full((1, LANES), masked_score, F32), unroll=True)

            def mix(step, kept):
                total, acc = kept
                at = pl.ds(pl.multiple_of((first + step * SLOTS) * BLOCK, BLOCK), WIDE)
                weights = jnp.exp(s_ref[step] - top)
                return (
                    total + jnp.sum(weights, axis=0, keepdims=True),
                    acc + rows_dot(weights.astype(BF), kv_ref[at, VALUE]),
                )

            total, acc = lax.fori_loop(0, CHUNKS, mix, (jnp.zeros((1, LANES), F32), jnp.zeros((LANES, LANES), F32)), unroll=True)
            scale = jnp.transpose(jnp.broadcast_to(1.0 / total, (LANES, LANES)))
            o_ref[rows, :] = join_pair(acc * scale).astype(BF)

        return carry

    lax.fori_loop(0, own_blocks, whole, 0)


def backward_kernel(
    heads, own_blocks, near_ref, rand_ref, glob_ref, q_ref, kv_ref, c_ref,
    dq_ref, dkv_ref, sum_ref, dk_acc, dv_acc, s_ref, p_ref,
):
    pair = pl.program_id(0)
    dk_acc[...] = jnp.zeros_like(dk_acc)
    dv_acc[...] = jnp.zeros_like(dv_acc)
    half = low_half()

    def add_rows(acc, shared, chosen, update):
        for i, position in enumerate(shared):
            at = pl.ds(pl.multiple_of(position * BLOCK, BLOCK), BLOCK)
            acc[at, :] += update[i * BLOCK : (i + 1) * BLOCK]
        for i, (one, two) in enumerate(chosen):
            piece = update[(5 + i) * BLOCK : (6 + i) * BLOCK]
            at = pl.ds(pl.multiple_of(one * BLOCK, BLOCK), BLOCK)
            acc[at, :] += jnp.where(half, piece, 0.0)
            at = pl.ds(pl.multiple_of(two * BLOCK, BLOCK), BLOCK)
            acc[at, :] += jnp.where(half, 0.0, piece)

    def regular(block, carry):
        rows = pl.ds(pl.multiple_of(block * BLOCK, BLOCK), BLOCK)
        shared, chosen = slots_of(near_ref, rand_ref, block, pair, heads)
        queries = split_pair(q_ref[rows, :] * 0.125)
        slope = c_ref[rows, :]
        slope = split_pair(jnp.where(glob_ref[block * 4] > 0, jnp.zeros_like(slope), slope))
        keys = slot_rows(kv_ref, KEY, shared, chosen)
        scores = masked(cols_dot(keys, queries), near_ref, block)
        weights = jnp.exp(scores - jnp.max(scores, axis=0, keepdims=True))
        probs = weights * (1.0 / jnp.sum(weights, axis=0, keepdims=True))
        dprobs = cols_dot(slot_rows(kv_ref, VALUE, shared, chosen), slope)
        inner = jnp.sum(probs * dprobs, axis=0, keepdims=True)
        dscores = (probs * (dprobs - inner)).astype(BF)
        dq_ref[rows, :] = (join_pair(rows_dot(dscores, keys)) * 0.125).astype(BF)
        add_rows(dk_acc, shared, chosen, plain_dot(dscores, queries))
        add_rows(dv_acc, shared, chosen, plain_dot(probs.astype(BF), slope))
        return carry

    lax.fori_loop(0, own_blocks, regular, 0, unroll=own_blocks)

    def whole(block, carry):
        @pl.when(glob_ref[block * 4] > 0)
        def _():
            rows = pl.ds(pl.multiple_of(block * BLOCK, BLOCK), BLOCK)
            first = glob_ref[block * 4 + 1]
            length = glob_ref[block * 4 + 2]
            queries = split_pair(q_ref[rows, :] * 0.125)
            slope = split_pair(c_ref[rows, :])
            slot_id = lax.broadcasted_iota(jnp.int32, (WIDE, LANES), 0) // BLOCK

            def score(step, top):
                at = pl.ds(pl.multiple_of((first + step * SLOTS) * BLOCK, BLOCK), WIDE)
                scores = cols_dot(kv_ref[at, KEY], queries)
                scores = jnp.where(slot_id < length - step * SLOTS, scores, masked_score)
                s_ref[step] = scores
                p_ref[step] = cols_dot(kv_ref[at, VALUE], slope)
                return jnp.maximum(top, jnp.max(scores, axis=0, keepdims=True))

            top = lax.fori_loop(0, CHUNKS, score, jnp.full((1, LANES), masked_score, F32), unroll=True)

            def weigh(step, kept):
                total, inner = kept
                weights = jnp.exp(s_ref[step] - top)
                s_ref[step] = weights
                return (
                    total + jnp.sum(weights, axis=0, keepdims=True),
                    inner + jnp.sum(weights * p_ref[step], axis=0, keepdims=True),
                )

            zero_row = jnp.zeros((1, LANES), F32)
            total, inner = lax.fori_loop(0, CHUNKS, weigh, (zero_row, zero_row), unroll=True)
            scale = 1.0 / total
            inner = inner * scale

            def spread(step, dq_sum):
                at = pl.ds(pl.multiple_of((first + step * SLOTS) * BLOCK, BLOCK), WIDE)
                probs = s_ref[step] * scale
                dscores = (probs * (p_ref[step] - inner)).astype(BF)
                dk_acc[at, :] += plain_dot(dscores, queries)
                dv_acc[at, :] += plain_dot(probs.astype(BF), slope)
                return dq_sum + rows_dot(dscores, kv_ref[at, KEY])

            dq_sum = lax.fori_loop(0, CHUNKS, spread, jnp.zeros((LANES, LANES), F32), unroll=True)
            dq_ref[rows, :] = (join_pair(dq_sum) * 0.125).astype(BF)

        return carry

    lax.fori_loop(0, own_blocks, whole, 0)
    dkv_ref[:, KEY] = dk_acc[...].astype(BF)
    dv_low = dv_acc[...].astype(BF)
    dkv_ref[:, VALUE] = dv_low
    sum_ref[0:1, :] = jnp.sum(dq_ref[...].astype(F32), axis=0, keepdims=True)
    sum_ref[1:2, :] = jnp.sum(dv_low.astype(F32), axis=0, keepdims=True)


def attention_calls(row_count, model_width, heads, buf_rows):
    own_blocks = row_count // BLOCK
    pairs = heads // 2
    own = lambda: pl.BlockSpec((row_count, LANES), lambda p, *_: (0, p))
    both = lambda: pl.BlockSpec((buf_rows, 2 * LANES), lambda p, *_: (0, p))
    params = lambda: pltpu.CompilerParams(vmem_limit_bytes=48 * 1024 * 1024)
    forward = pl.pallas_call(
        functools.partial(forward_kernel, heads, own_blocks),
        out_shape=jax.ShapeDtypeStruct((row_count, model_width), BF),
        grid_spec=pltpu.PrefetchScalarGridSpec(
            num_scalar_prefetch=3,
            grid=(pairs,),
            in_specs=[own(), both()],
            out_specs=own(),
            scratch_shapes=[pltpu.VMEM((CHUNKS, WIDE, LANES), F32)],
        ),
        compiler_params=params(),
        cost_estimate=pl.CostEstimate(
            flops=4 * row_count * WIDE * 2 * model_width, bytes_accessed=4 * buf_rows * model_width,
            transcendentals=row_count * WIDE * heads,
        ),
        name="attend_forward",
    )
    backward = pl.pallas_call(
        functools.partial(backward_kernel, heads, own_blocks),
        out_shape=(
            jax.ShapeDtypeStruct((row_count, model_width), BF),
            jax.ShapeDtypeStruct((buf_rows, 2 * model_width), BF),
            jax.ShapeDtypeStruct((2, model_width), F32),
        ),
        grid_spec=pltpu.PrefetchScalarGridSpec(
            num_scalar_prefetch=3,
            grid=(pairs,),
            in_specs=[own(), both(), own()],
            out_specs=[own(), both(), pl.BlockSpec((2, LANES), lambda p, *_: (0, p))],
            scratch_shapes=[
                pltpu.VMEM((buf_rows, LANES), F32),
                pltpu.VMEM((buf_rows, LANES), F32),
                pltpu.VMEM((CHUNKS, WIDE, LANES), F32),
                pltpu.VMEM((CHUNKS, WIDE, LANES), F32),
            ],
        ),
        compiler_params=params(),
        cost_estimate=pl.CostEstimate(
            flops=10 * row_count * WIDE * 2 * model_width, bytes_accessed=8 * buf_rows * model_width,
            transcendentals=row_count * WIDE * heads,
        ),
        name="attend_backward",
    )
    return forward, backward


def interleaved(one, two):
    return jnp.concatenate(
        [side[..., i : i + LANES] for i in range(0, one.shape[-1], LANES) for side in (one, two)], axis=-1
    )


def on_device(
    layer_input, out_grad, doc_starts, rand_blocks, query_weight, query_bias, key_weight, value_weight,
    value_bias, output_weight, output_bias, first_gain, first_shift, inner_weight, inner_bias,
    outer_weight, outer_bias, second_gain, second_shift,
):
    row_count, model_width = layer_input.shape
    head_count = rand_blocks.shape[1]
    devices = lax.axis_size("ctx")
    own_blocks = row_count // BLOCK
    buf_blocks = 2 * REACH + own_blocks
    own_first = lax.axis_index("ctx") * own_blocks
    buf_first = own_first - REACH
    block_total = own_blocks * devices
    own_ids = own_first + jnp.arange(own_blocks, dtype=jnp.int32)
    own_doc, own_start = doc_layout(doc_starts, own_ids)
    next_doc = doc_layout(doc_starts, own_ids + 1)[0]
    start_blocks = doc_starts // BLOCK
    later = start_blocks[None, :] > own_ids[:, None]
    doc_end = jnp.min(jnp.where(later, start_blocks[None, :], block_total), axis=1)
    glob_own = own_ids - own_start < 2

    def local(ids):
        return jnp.clip(ids - buf_first, 0, buf_blocks - 1).astype(jnp.int32)

    near = jnp.stack(
        [
            local(own_ids - 1),
            local(own_ids),
            local(own_ids + 1),
            local(own_start),
            local(own_start + 1),
            ((own_ids + 1 < block_total) & (next_doc == own_doc)).astype(jnp.int32),
            (own_ids - own_start > 2).astype(jnp.int32),
            jnp.zeros_like(own_ids),
        ],
        axis=1,
    ).reshape(-1)
    picks = local(rand_blocks).reshape(-1)
    spans = jnp.stack(
        [glob_own.astype(jnp.int32), local(own_start), doc_end - own_start, jnp.zeros_like(own_ids)], axis=1
    ).reshape(-1)
    attend, attend_back = attention_calls(row_count, model_width, head_count, buf_blocks * BLOCK)
    m = model_width
    unit = query_bias.shape[0]
    weight_rows = query_weight.shape[0]

    def gathered(value):
        return lax.all_gather(value, "ctx", axis=0, tiled=True)

    vectors = jnp.concatenate(
        [
            query_bias, value_bias, output_bias, first_gain, first_shift, outer_bias, second_gain, second_shift,
            inner_bias,
        ]
    )
    lane_pad = -vectors.shape[0] % LANES
    first_all, vector_all, x_buf = gather_weights(
        query_weight, key_weight, value_weight, jnp.pad(vectors, (0, lane_pad))[None, :], layer_input, devices
    )
    w_qkv = first_all.reshape(m, 3 * m)
    vector_all = vector_all[:, 0].astype(F32)
    b_query, b_value, b_output, g_first, s_first, b_outer, g_second, s_second = [
        vector_all[:, i * unit : (i + 1) * unit].reshape(-1) for i in range(8)
    ]
    b_inner = vector_all[:, 8 * unit : 8 * unit + inner_bias.shape[0]].reshape(-1)
    outer_rows = outer_weight.shape[0]
    hidden_blocks = inner_weight.shape[1] // m
    late = gathered(
        jnp.concatenate(
            [outer_weight, output_weight] + [inner_weight[:, i * m : (i + 1) * m] for i in range(hidden_blocks)], axis=0
        ).astype(BF)[None]
    )
    w_outer = late[:, :outer_rows].reshape(-1, m)
    w_output, *w_inner = [
        late[:, outer_rows + i * weight_rows : outer_rows + (i + 1) * weight_rows].reshape(m, m)
        for i in range(1 + hidden_blocks)
    ]
    w_inner = jnp.concatenate(w_inner, axis=1)
    w_query, w_kv = w_qkv[:, :m], w_qkv[:, m:]

    query_rows = (plain_dot(layer_input, w_query) + b_query).astype(BF)
    kv_buf = (plain_dot(x_buf, w_kv) + interleaved(jnp.zeros_like(b_value), b_value)).astype(BF)
    context_rows = attend(near, picks, spans, query_rows, kv_buf)

    input_float = layer_input.astype(F32)
    resid_one = input_float + plain_dot(context_rows, w_output) + b_output
    normed_one, first_pull = jax.vjp(layer_norm, resid_one, g_first, s_first)
    normed_low = normed_one.astype(BF)
    inner_pre = plain_dot(normed_low, w_inner) + b_inner
    active, active_slope = gelu_and_slope(inner_pre)
    active, active_slope = lax.optimization_barrier((active.astype(BF), active_slope))
    resid_two = normed_one + plain_dot(active, w_outer) + b_outer
    normed_two, second_pull = jax.vjp(layer_norm, resid_two, g_second, s_second)
    layer_out = normed_two.astype(BF)

    def scattered(value):
        return lax.psum_scatter(value, "ctx", scatter_dimension=0, tiled=True).astype(F32)

    grad_two, grad_second_gain, grad_second_shift = second_pull(out_grad.astype(F32))
    grad_two_low = grad_two.astype(BF)
    grad_outer_bias = jnp.sum(grad_two_low.astype(F32), axis=0)
    grad_outer_weight = rows_dot(active, grad_two_low).astype(BF)
    grad_inner = (cols_dot(grad_two_low, w_outer) * active_slope).astype(BF)
    grad_inner_bias = jnp.sum(grad_inner.astype(F32), axis=0)
    grad_inner_weight = rows_dot(normed_low, grad_inner).astype(BF)
    grad_one = grad_two + cols_dot(grad_inner, w_inner)
    grad_resid_one, grad_first_gain, grad_first_shift = first_pull(grad_one)
    grad_one_low = grad_resid_one.astype(BF)
    grad_output_bias = jnp.sum(grad_one_low.astype(F32), axis=0)
    grad_output_weight = rows_dot(context_rows, grad_one_low).astype(BF)
    slabs = lambda value: value.reshape(devices, -1, m)
    late_grads = scattered(
        jnp.concatenate(
            [slabs(grad_outer_weight), slabs(grad_output_weight)]
            + [slabs(grad_inner_weight[:, i * m : (i + 1) * m]) for i in range(hidden_blocks)],
            axis=1,
        )
    )[0]
    grad_outer_weight = late_grads[:outer_rows]
    late_grads = late_grads[outer_rows:].reshape(1 + hidden_blocks, weight_rows, m)
    grad_output_weight = late_grads[0]
    grad_inner_weight = jnp.concatenate([late_grads[1 + i] for i in range(hidden_blocks)], axis=1)
    context_gradient = cols_dot(grad_one_low, w_output).astype(BF)

    query_low, kv_low, attn_sums = attend_back(near, picks, spans, query_rows, kv_buf, context_gradient)
    grad_x_buf = cols_dot(kv_low, w_kv).astype(BF)
    grad_vectors = jnp.concatenate(
        [
            attn_sums,
            jnp.stack(
                [
                    grad_output_bias, grad_first_gain, grad_first_shift, grad_outer_bias, grad_second_gain,
                    grad_second_shift,
                ]
            ),
            grad_inner_bias.reshape(-1, m),
        ],
        axis=0,
    )
    grad_query_weight, grad_key_weight, grad_value_weight, sums, halo_part = reduce_grads(
        rows_dot(layer_input, query_low).astype(BF).reshape(devices, -1, m),
        rows_dot(x_buf, kv_low).astype(BF).reshape(devices, -1, 2 * m),
        grad_vectors,
        grad_x_buf,
        row_count,
        devices,
    )
    grad_input = grad_resid_one + cols_dot(query_low, w_query) + halo_part
    me = lax.axis_index("ctx")
    own_sums = lax.dynamic_slice_in_dim(sums[:8], me * unit, unit, 1)
    v_query, v_value, v_output, v_gain1, v_shift1, v_outer, v_gain2, v_shift2 = [own_sums[i] for i in range(8)]
    inner_unit = inner_bias.shape[0]
    inner_at = me * inner_unit
    v_inner = lax.dynamic_slice(sums, (8 + inner_at // m, inner_at % m), (1, inner_unit))[0]
    return (
        layer_out, grad_input, grad_query_weight, v_query, grad_key_weight, grad_value_weight, v_value,
        grad_output_weight, v_output, v_gain1, v_shift1, grad_inner_weight, v_inner, grad_outer_weight, v_outer,
        v_gain2, v_shift2,
    )


def solution(mesh):
    rows, line = P("ctx", None), P("ctx")
    in_specs = (
        rows, rows, P(), P("ctx", None, None), rows, line, rows, rows, line, rows, line, line, line, rows, line, rows,
        line, line, line,
    )
    out_specs = (
        rows, rows, rows, line, rows, rows, line, rows, line, line, line, rows, line, rows, line, line, line,
    )
    return jax.shard_map(on_device, mesh=mesh, in_specs=in_specs, out_specs=out_specs, check_vma=False)
```
